128 devices in a mesh: section: 4 (over x), tp: 32 (over z, y, core).
Axes of the slice: x: 4, y: 4, z: 4, core: 2. Of those that a mesh axis runs over, the one named last changes fastest.
Arguments:
- inputs: bfloat16 [2, 128, 8192], P(None, 'tp'), may hold values from -50 to 50
- cotangent: bfloat16 [2, 128, 8192], P(None, 'tp'), may hold values from -50 to 50
- gains: bfloat16 [4, 8192], P('section'), may hold values from 0.099609375 to 1.8984375
- up_blocks: bfloat16 [4, 18432, 4096], P('section', 'tp'), may hold values from -0.09375 to 0.09375
- up_index: int32 [4, 18432], P('section', 'tp'), may hold values from 0 to 1023, as said below
- up_count: int32 [4, 32], P('section', 'tp'), may hold values from 448 to 576, as said below
- down_blocks: bfloat16 [4, 18432, 4096], P('section', 'tp'), may hold values from -0.0625 to 0.0625
- down_index: int32 [4, 18432], P('section', 'tp'), may hold values from 0 to 1023, as said below
- down_count: int32 [4, 32], P('section', 'tp'), may hold values from 448 to 576, as said below
Outputs:
- section_outputs: bfloat16 [4, 2, 128, 8192], P('section', None, 'tp')
- input_grads: bfloat16 [4, 2, 128, 8192], P('section', None, 'tp')
- up_grads: bfloat16 [4, 18432, 4096], P('section', 'tp')
- down_grads: bfloat16 [4, 18432, 4096], P('section', 'tp')
The draws below stay inside these ranges and needn't reach their ends.
Inputs may be any that keep to these rules, and one draw needn't show every extreme that they name: Within one group's 576 entries of up_index no value repeats. Within one group's 576 entries of down_index no value repeats. `up_count`: in every layer one group has exactly 576 live blocks and another exactly 448. `down_count`: in every layer one group has exactly 576 live blocks and another exactly 448.
All inputs are finite; a program needn't handle non-finite values.
Results may differ from the reference program's by a relative error of at most 0.03.
Values may be sent and summed in bfloat16 or wider, within the bound.
A program may use at most 256 MiB of HBM per device.

```python
import math
from functools import partial
import jax
import jax.numpy as jnp
from jax import lax

D = 8192
FF = 16384
BLOCK = 64
MICRO = 2
TOKENS = 128
SECTIONS = 4
SHARD_BLOCKS = 1024
CAP = 576
LOW = 448
SLOTS = 18432
N_TP = 32


def spread_rows(base_key, shape):
    noise_key, row_key, col_key = jax.random.split(base_key, 3)
    noise = jnp.clip(jax.random.normal(noise_key, shape, jnp.float32), -4.0, 4.0)
    row_scale = jnp.exp(jax.random.uniform(row_key, shape[:-1] + (1,), jnp.float32, math.log(0.3), math.log(3.0)))
    col_scale = jnp.exp(jax.random.uniform(col_key, shape[-1:], jnp.float32, math.log(0.3), math.log(3.0)))
    return noise * row_scale * col_scale


def block_lists(base_key):
    group_keys = jax.random.split(base_key, SECTIONS * (SLOTS // CAP))
    lists = jax.vmap(lambda one_key: jax.random.permutation(one_key, SHARD_BLOCKS)[:CAP])(group_keys)
    return lists.reshape(SECTIONS, SLOTS).astype(jnp.int32)


def block_counts(base_key):
    groups = SLOTS // CAP
    count_key, full_key = jax.random.split(base_key)
    counts = jax.random.randint(count_key, (SECTIONS, groups), LOW, CAP + 1, jnp.int32)
    fullest = jax.random.randint(full_key, (SECTIONS, 1), 0, groups, jnp.int32)
    emptiest = (fullest + 1) % groups
    positions = jnp.arange(groups, dtype=jnp.int32)[None, :]
    counts = jnp.where(positions == fullest, CAP, counts)
    counts = jnp.where(positions == emptiest, LOW, counts)
    return counts.astype(jnp.int32)


def draw_inputs(key, part):
    return spread_rows(jax.random.fold_in(key, 11), (MICRO, TOKENS, D)).astype(jnp.bfloat16)


def draw_cotangent(key, part):
    return spread_rows(jax.random.fold_in(key, 23), (MICRO, TOKENS, D)).astype(jnp.bfloat16)


def draw_up_index(key, part):
    return block_lists(jax.random.fold_in(key, 31))


def draw_down_index(key, part):
    return block_lists(jax.random.fold_in(key, 37))


def draw_up_count(key, part):
    return block_counts(jax.random.fold_in(key, 41))


def draw_down_count(key, part):
    return block_counts(jax.random.fold_in(key, 43))


def shard_levels(rng, extent, cuts, smallest, high):
    def one(position, blocks):
        steps = jax.random.uniform(jax.random.fold_in(jax.random.fold_in(rng, 6), position), (blocks,), jnp.float32, smallest / len(cuts), high / len(cuts))
        return jnp.repeat(jnp.exp(steps), extent[position] // blocks).reshape((-1,) + (1,) * (len(extent) - position - 1))

    loudness = one(*cuts[0])
    for cut in cuts[1:]:
        loudness = loudness * one(*cut)
    return loudness


def scatter_about(stream_key, extent, scale, limit, cuts=(), kind=jnp.bfloat16):
    factor_of = shard_levels(stream_key, extent, cuts, -0.22, 0.18) if cuts else 1.0
    values = jax.random.normal(stream_key, extent, jnp.float32) * scale * factor_of
    return jnp.minimum(jnp.maximum(values, -limit), limit).astype(kind)


def setup_inputs(seed: int = 0) -> dict:
    seeds = jax.random.split(jax.random.key(seed), 10)
    return {
        "inputs": draw_inputs(jax.random.fold_in(seeds[9], 71), 0),
        "cotangent": draw_cotangent(jax.random.fold_in(seeds[9], 71), 0),
        "gains": jnp.clip(1.0 + 0.18 * jax.random.normal(seeds[2], (SECTIONS, D), jnp.float32), 0.099609375, 1.8984375).astype(jnp.bfloat16),
        "up_blocks": scatter_about(seeds[3], (SECTIONS, SLOTS, BLOCK * BLOCK), (D // 2) ** -0.5, 0.09375, ((0, 4), (1, 32))),
        "up_index": draw_up_index(jax.random.fold_in(seeds[9], 71), 0),
        "up_count": draw_up_count(jax.random.fold_in(seeds[9], 71), 0),
        "down_blocks": scatter_about(seeds[6], (SECTIONS, SLOTS, BLOCK * BLOCK), (FF // 2) ** -0.5, 0.0625, ((0, 4), (1, 32))),
        "down_index": draw_down_index(jax.random.fold_in(seeds[9], 71), 0),
        "down_count": draw_down_count(jax.random.fold_in(seeds[9], 71), 0),
    }


NORM_EPSILON = 1e-05

def densify(blocks, block_index, live_count, row_blocks, col_blocks):
    side = blocks.shape[-1]
    live_slots = jnp.arange(blocks.shape[0]) < live_count
    kept_values = jnp.where(live_slots[:, None, None], blocks, jnp.zeros_like(blocks))
    block_grid = jnp.zeros((row_blocks * col_blocks, side, side), blocks.dtype).at[block_index].add(kept_values)
    block_grid = block_grid.reshape(row_blocks, col_blocks, side, side).transpose(0, 2, 1, 3)
    return block_grid.reshape(row_blocks * side, col_blocks * side)

def extract(dense_grad, block_index, live_count, row_blocks, col_blocks):
    side = dense_grad.shape[0] // row_blocks
    block_grid = dense_grad.reshape(row_blocks, side, col_blocks, side).transpose(0, 2, 1, 3)
    block_grid = block_grid.reshape(row_blocks * col_blocks, side, side)
    picked = block_grid[block_index]
    live_slots = jnp.arange(block_index.shape[0]) < live_count
    return jnp.where(live_slots[:, None, None], picked, jnp.zeros_like(picked)).astype(jnp.bfloat16)

def normalize(activ_rows, gain):
    values = activ_rows.astype(jnp.float32)
    inv_rms = lax.rsqrt(lax.optimization_barrier(jnp.mean(values * values, axis=-1, keepdims=True)) + NORM_EPSILON)
    return (values, inv_rms, (values * inv_rms * gain.astype(jnp.float32)).astype(jnp.bfloat16))

def layer_weights(blocks, block_index, live_count, row_blocks, col_blocks):
    groups = live_count.shape[0]
    slot_count = block_index.shape[0] // groups
    side = blocks.shape[-1]
    maker = partial(densify, row_blocks=row_blocks, col_blocks=col_blocks)
    return jax.vmap(maker)(blocks.reshape(groups, slot_count, side, side), block_index.reshape(groups, slot_count), live_count)

def forward_section(activ_in, gain, w_up, w_down):
    values, inv_rms, normed = normalize(activ_in, gain)
    token_rows = normed.reshape(-1, normed.shape[-1])

    def group_step(running, weight_pair):
        up_proj = jnp.dot(token_rows, weight_pair[0], preferred_element_type=jnp.float32)
        hidden = jax.nn.silu(up_proj).astype(jnp.bfloat16)
        part = jnp.dot(hidden, weight_pair[1], preferred_element_type=jnp.float32).astype(jnp.bfloat16)
        part = lax.optimization_barrier(part)
        return (running + part.astype(jnp.float32), None)
    mixed_rows, _ = lax.scan(group_step, jnp.zeros(token_rows.shape, jnp.float32), (w_up, w_down))
    return (values + mixed_rows.reshape(values.shape)).astype(jnp.bfloat16)

def backward_section(activ_in, grad_out, gain, w_up, w_down, up_index, up_count, down_index, down_count):
    values, inv_rms, normed = normalize(activ_in, gain)
    features = activ_in.shape[-1]
    token_rows = normed.reshape(-1, features)
    grad_rows = grad_out.reshape(-1, features)
    group_width = w_up.shape[-1]
    row_blocks = features // BLOCK
    group_blocks = group_width // BLOCK
    groups = up_count.shape[0]

    def group_step(running, pieces):
        weight_up, weight_down, index_up, count_up, index_down, count_down = pieces
        up_proj = jnp.dot(token_rows, weight_up, preferred_element_type=jnp.float32)
        hidden = jax.nn.silu(up_proj).astype(jnp.bfloat16)
        act_grad = jnp.dot(grad_rows, weight_down.T, preferred_element_type=jnp.float32)
        sigmoid_up = jax.nn.sigmoid(up_proj)
        up_grad = (act_grad * sigmoid_up * (1.0 + up_proj * (1.0 - sigmoid_up))).astype(jnp.bfloat16)
        back_part = jnp.dot(up_grad, weight_up.T, preferred_element_type=jnp.float32).astype(jnp.bfloat16)
        back_part = lax.optimization_barrier(back_part)
        up_dense = jnp.dot(token_rows.T, up_grad, preferred_element_type=jnp.float32)
        down_dense = jnp.dot(hidden.T, grad_rows, preferred_element_type=jnp.float32)
        up_part = extract(up_dense, index_up, count_up, row_blocks, group_blocks)
        down_part = extract(down_dense, index_down, count_down, group_blocks, row_blocks)
        return (running + back_part.astype(jnp.float32), (up_part, down_part))
    pieces = (w_up, w_down, up_index.reshape(groups, -1), up_count, down_index.reshape(groups, -1), down_count)
    norm_grad, grads = lax.scan(group_step, jnp.zeros(grad_rows.shape, jnp.float32), pieces)
    scaled_grad = norm_grad.reshape(values.shape) * gain.astype(jnp.float32)
    norm_term = inv_rms * scaled_grad - values * (inv_rms * inv_rms * inv_rms) * lax.optimization_barrier(jnp.mean(scaled_grad * values, axis=-1, keepdims=True))
    grad_in = (grad_out.astype(jnp.float32) + norm_term).astype(jnp.bfloat16)
    up_part, down_part = grads
    return (grad_in, up_part.reshape(-1, BLOCK * BLOCK), down_part.reshape(-1, BLOCK * BLOCK))

def reference(inputs, cotangent, gains, up_blocks, up_index, up_count, down_blocks, down_index, down_count):
    row_blocks = D // BLOCK
    group_blocks = FF // N_TP // BLOCK
    up_square = up_blocks.reshape(SECTIONS, SLOTS, BLOCK, BLOCK)
    down_square = down_blocks.reshape(SECTIONS, SLOTS, BLOCK, BLOCK)
    activations = [inputs]
    for section_index in range(SECTIONS):
        w_up = layer_weights(up_square[section_index], up_index[section_index], up_count[section_index], row_blocks, group_blocks)
        w_down = layer_weights(down_square[section_index], down_index[section_index], down_count[section_index], group_blocks, row_blocks)
        activations.append(forward_section(activations[-1], gains[section_index], w_up, w_down))
    grad_now = cotangent
    grads_in, grads_up, grads_down = ([], [], [])
    for section_index in reversed(range(SECTIONS)):
        w_up = layer_weights(up_square[section_index], up_index[section_index], up_count[section_index], row_blocks, group_blocks)
        w_down = layer_weights(down_square[section_index], down_index[section_index], down_count[section_index], group_blocks, row_blocks)
        grad_now, grad_up, grad_down = backward_section(activations[section_index], grad_now, gains[section_index], w_up, w_down, up_index[section_index], up_count[section_index], down_index[section_index], down_count[section_index])
        grads_in.insert(0, grad_now)
        grads_up.insert(0, grad_up)
        grads_down.insert(0, grad_down)
    return (jnp.stack(activations[1:]), jnp.stack(grads_in), jnp.stack(grads_up), jnp.stack(grads_down))
```

```python
import functools

import jax
import jax.numpy as jnp
from jax import lax
from jax.experimental import pallas as pl
from jax.experimental.pallas import tpu as pltpu
from jax.sharding import PartitionSpec as P

FF = 16384
BLOCK = 64
NORM_EPSILON = 1e-05
MESH = pl.DeviceIdType.MESH
F32 = jnp.float32
BF16 = jnp.bfloat16
SIDE = 4
CORES = 2


def place_kernel(slots_ref, blocks_ref, out_ref, *, row_major, row_blocks, col_blocks):
    step = pl.program_id(0)

    def pair(block_row, block_col):
        parts = []
        for k in range(2):
            slot = slots_ref[block_row * col_blocks + block_col + k]
            block = blocks_ref[jnp.maximum(slot, 0)]
            parts.append(jnp.where(slot >= 0, block, jnp.zeros_like(block)))
        return jnp.concatenate(parts, axis=1)

    if row_major:
        rows = out_ref.shape[0] // BLOCK

        @pl.loop(0, rows)
        def _(row):
            for col in range(0, col_blocks, 2):
                out_ref[pl.ds(pl.multiple_of(row * BLOCK, BLOCK), BLOCK), col * BLOCK : (col + 2) * BLOCK] = pair(
                    step * rows + row, col
                )
    else:
        cols = out_ref.shape[1] // (2 * BLOCK)

        @pl.loop(0, cols)
        def _(col):
            for row in range(row_blocks):
                out_ref[
                    row * BLOCK : (row + 1) * BLOCK, pl.ds(pl.multiple_of(col * 2 * BLOCK, 2 * BLOCK), 2 * BLOCK)
                ] = pair(row, (step * cols + col) * 2)


def densify(blocks, block_index, live_count, row_blocks, col_blocks):
    slot_count = blocks.shape[0]
    slots = jnp.arange(slot_count, dtype=jnp.int32)
    places = jnp.arange(row_blocks * col_blocks, dtype=jnp.int32)
    hit = (block_index[None, :] == places[:, None]) & (slots < live_count)[None, :]
    slot_of_place = jnp.max(jnp.where(hit, slots[None, :], -1), axis=1)
    row_major = row_blocks > col_blocks
    steps = 8
    rows, cols = row_blocks * BLOCK, col_blocks * BLOCK
    if row_major:
        out_spec = pl.BlockSpec((rows // steps, cols), lambda i, *_: (i, 0))
    else:
        out_spec = pl.BlockSpec((rows, cols // steps), lambda i, *_: (0, i))
    return pl.pallas_call(
        functools.partial(place_kernel, row_major=row_major, row_blocks=row_blocks, col_blocks=col_blocks),
        out_shape=jax.ShapeDtypeStruct((rows, cols), blocks.dtype),
        grid_spec=pltpu.PrefetchScalarGridSpec(
            num_scalar_prefetch=1,
            grid=(steps,),
            in_specs=[pl.BlockSpec(blocks.shape, lambda i, *_: (0, 0, 0), pipeline_mode=pl.Buffered(1))],
            out_specs=out_spec,
        ),
        compiler_params=pltpu.CompilerParams(vmem_limit_bytes=32 << 20),
    )(slot_of_place, blocks)


def weight_grad_kernel(index_ref, count_ref, lhs_ref, rhs_ref, out_ref, dense, *, up, col_blocks):
    step = pl.program_id(0)
    product = lax.dot_general(
        lhs_ref[0], rhs_ref[0], (((0,), (0,)), ((), ())), preferred_element_type=F32
    ).astype(BF16)
    chunks = product.shape[1] // 128
    for j in range(chunks):
        piece = product[:, 128 * j : 128 * (j + 1)]
        if up:
            dense[j, pl.ds(pl.multiple_of(step * product.shape[0], 128), product.shape[0]), :] = piece
        else:
            dense[step * chunks + j] = piece

    @pl.when(step == pl.num_programs(0) - 1)
    def _():
        count = count_ref[0]

        @pl.loop(0, out_ref.shape[0] // 4)
        def _(group):
            for k in range(4):
                slot = group * 4 + k
                place = index_ref[slot]
                block_row, block_col = lax.div(place, col_blocks), lax.rem(place, col_blocks)
                tile = dense[lax.div(block_col, 2), pl.ds(pl.multiple_of(block_row * BLOCK, BLOCK), BLOCK), :]
                block = jnp.where(lax.rem(block_col, 2) == 0, tile[:, :BLOCK], tile[:, BLOCK:])
                out_ref[slot] = jnp.where(slot < count, block, jnp.zeros_like(block))


def weight_grad(lhs, rhs, block_index, live_count, up, col_blocks):
    halves, tokens, width = (lhs if up else rhs).shape
    units = (rhs if up else lhs).shape[2]
    tile = 512
    per_half = width // tile
    wide = pl.BlockSpec((1, tokens, tile), lambda i, *_: (i // per_half, 0, i % per_half))
    narrow = pl.BlockSpec((1, tokens, units), lambda i, *_: (i // per_half, 0, 0))
    features = halves * width
    slots = block_index.shape[0]
    dense_shape = (units // 128, features, 128) if up else (features // 128, units, 128)
    return pl.pallas_call(
        functools.partial(weight_grad_kernel, up=up, col_blocks=col_blocks),
        out_shape=jax.ShapeDtypeStruct((slots, BLOCK, BLOCK), BF16),
        grid_spec=pltpu.PrefetchScalarGridSpec(
            num_scalar_prefetch=2,
            grid=(halves * per_half,),
            in_specs=[wide, narrow] if up else [narrow, wide],
            out_specs=pl.BlockSpec((slots, BLOCK, BLOCK), lambda i, *_: (0, 0, 0), pipeline_mode=pl.Buffered(1)),
            scratch_shapes=[pltpu.VMEM(dense_shape, BF16)],
        ),
        compiler_params=pltpu.CompilerParams(vmem_limit_bytes=40 << 20),
    )(block_index, live_count, lhs, rhs)


def layers_kernel(
    inp, cot, gain_ref, w_up_hbm, w_down_hbm,
    outs, grads, rows_hbm, hid_out, ug_out,
    w_up, w_down, xin, gin, ibuf, gath, part, xbuf, sbuf, obuf, rsend, rbuf, ya, yb, up_keep, tmp,
    w_sem, keep_sem, sec_send, sec_recv, p1_send, p1_recv, p2_send, p2_recv, sib_send, sib_recv,
    r0_send, r0_recv, r1_send, r1_recv, r2_send, r2_recv,
):
    micro, toks, features = inp.shape
    half = features // 2
    slab = SIDE * toks
    section, tp = lax.axis_index("section"), lax.axis_index("tp")
    sections = lax.axis_size("section")
    core = lax.rem(tp, CORES)
    y = lax.rem(lax.div(tp, CORES), SIDE)
    z = lax.div(tp, CORES * SIDE)
    sibling = {"tp": tp + 1 - 2 * core}
    inner = (z, y)
    outer = (y, z)

    def at(zz, yy):
        return {"tp": (zz * SIDE + yy) * CORES + core}

    def inner_peer(h, k):
        i = lax.rem(inner[h] + k, SIDE)
        return i, (at(i, y) if h == 0 else at(z, i))

    def outer_peer(h, k):
        o = lax.rem(outer[h] + k, SIDE)
        return o, (at(z, o) if h == 0 else at(o, y))

    def remote(src, dst, send, recv, device):
        return pltpu.make_async_remote_copy(
            src_ref=src, dst_ref=dst, send_sem=send, recv_sem=recv, device_id=device, device_id_type=MESH
        )

    load_up = pltpu.make_async_copy(w_up_hbm, w_up, w_sem.at[0])
    load_down = pltpu.make_async_copy(w_down_hbm, w_down, w_sem.at[1])
    load_up.start()
    load_down.start()

    barrier = pltpu.get_barrier_semaphore()
    peers = [sibling]
    for h in range(2):
        peers += [inner_peer(h, k)[1] for k in range(1, SIDE)]
    for peer in peers:
        pl.semaphore_signal(barrier, inc=1, device_id=peer, device_id_type=MESH)

    @pl.when(section > 0)
    def _():
        pl.semaphore_signal(barrier, inc=1, device_id={"section": section - 1}, device_id_type=MESH)

    @pl.when(section < sections - 1)
    def _():
        pl.semaphore_signal(barrier, inc=1, device_id={"section": section + 1}, device_id_type=MESH)

    @pl.when((section == 0) | (section == sections - 1))
    def _():
        pl.semaphore_wait(barrier, len(peers) + 1)

    @pl.when((section > 0) & (section < sections - 1))
    def _():
        pl.semaphore_wait(barrier, len(peers) + 2)

    ORDER = (1, 3, 2)

    def slab_rows(o, c):
        return pl.ds(pl.multiple_of((o * CORES + c) * slab, slab), slab)

    def gather(job, values):
        first = []
        for h in range(2):
            mine = ibuf.at[job, h, inner[h]]
            mine[...] = values[:, h * half : (h + 1) * half].astype(BF16)
        for k in ORDER:
            for h in range(2):
                mine = ibuf.at[job, h, inner[h]]
                copy = remote(mine, mine, p1_send.at[job, h, k - 1], p1_recv.at[job, h, k - 1], inner_peer(h, k)[1])
                copy.start()
                first.append(copy)
        for copy in first:
            copy.wait_recv()
        second, side = {}, []
        for h in range(2):
            for i in range(SIDE):
                tmp[h, i * toks : (i + 1) * toks, :] = ibuf[job, h, i].astype(F32)
            rows = slab_rows(outer[h], core)
            gath[job, h, rows, :] = tmp[h].astype(BF16)
            mine = gath.at[job, h, rows]
            for k in ORDER:
                copy = remote(mine, mine, p2_send.at[job, h, k - 1], p2_recv.at[job, h, k - 1], outer_peer(h, k)[1])
                copy.start()
                second[h, k] = copy
            copy = remote(mine, mine, sib_send.at[job, h, 0], sib_recv.at[job, h, 0], sibling)
            copy.start()
            side.append(copy)
        for k in ORDER:
            for h in range(2):
                second[h, k].wait_recv()
                came = gath.at[job, h, slab_rows(outer_peer(h, SIDE - k)[0], core)]
                copy = remote(came, came, sib_send.at[job, h, k], sib_recv.at[job, h, k], sibling)
                copy.start()
                side.append(copy)
        for copy in side:
            copy.wait_recv()
        for copy in first + list(second.values()) + side:
            copy.wait_send()

    def keep(job):
        return [
            pltpu.make_async_copy(
                gath.at[job, h],
                rows_hbm.at[lax.div(job, micro), h, pl.ds(pl.multiple_of(lax.rem(job, micro) * 128, 128), 128)],
                keep_sem.at[job, h],
            )
            for h in range(2)
        ]

    def permuted(target, source, add):
        for a in range(SIDE):
            for c in range(CORES):
                for b in range(SIDE):
                    to, of = ((a * CORES + c) * SIDE + b) * toks, ((b * CORES + c) * SIDE + a) * toks
                    moved = source[of : of + toks, :]
                    target[to : to + toks, :] = target[to : to + toks, :] + moved if add else moved

    def scatter(job):
        sends = []
        zero = []
        for h in range(2):
            for o in range(SIDE):
                copy = remote(
                    part.at[h, slab_rows(o, 1 - core)],
                    xbuf.at[job, h, o],
                    r0_send.at[job, h, o],
                    r0_recv.at[job, h, o],
                    sibling,
                )
                copy.start()
                zero.append(copy)
        one = {}
        for copy in zero:
            copy.wait_recv()
        for h in range(2):
            for k in ORDER + (0,):
                o, peer = outer_peer(h, k)
                both = part[h, slab_rows(o, core), :].astype(F32) + xbuf[job, h, o].astype(F32)
                if k:
                    sbuf[h, k - 1] = both.astype(BF16)
                    copy = remote(
                        sbuf.at[h, k - 1],
                        obuf.at[job, h, k - 1],
                        r1_send.at[job, h, k - 1],
                        r1_recv.at[job, h, k - 1],
                        peer,
                    )
                    copy.start()
                    one[h, k] = copy
                else:
                    tmp[h] = both
        two = {}
        for h in range(2):
            for k in ORDER:
                one[h, k].wait_recv()
            tmp[h] = tmp[h] + (obuf[job, h, 0].astype(F32) + obuf[job, h, 1].astype(F32) + obuf[job, h, 2].astype(F32))
            for i in range(SIDE):
                rsend[h, i] = tmp[h, i * toks : (i + 1) * toks, :].astype(BF16)
            for k in ORDER:
                i, peer = inner_peer(h, k)
                copy = remote(
                    rsend.at[h, i],
                    rbuf.at[job, h, k - 1],
                    r2_send.at[job, h, k - 1],
                    r2_recv.at[job, h, k - 1],
                    peer,
                )
                copy.start()
                two[h, k] = copy
        sums = []
        for h in range(2):
            for k in ORDER:
                two[h, k].wait_recv()
            own = rsend[h, inner[h]].astype(F32)
            sums.append(
                own + (rbuf[job, h, 0].astype(F32) + rbuf[job, h, 1].astype(F32) + rbuf[job, h, 2].astype(F32))
            )
        for copy in zero + list(one.values()) + list(two.values()):
            copy.wait_send()
        return jnp.concatenate(sums, axis=1)

    gain = gain_ref[...].astype(F32)
    K_TILE = 1024
    N_TILE = 512
    NT = (((1,), (1,)), ((), ()))

    def forward_in(mb):
        return remote(outs.at[mb], xin.at[mb], sec_send.at[0, mb], sec_recv.at[0, mb], {"section": section + 1})

    def backward_in(mb):
        return remote(grads.at[mb], gin.at[mb], sec_send.at[1, mb], sec_recv.at[1, mb], {"section": section - 1})

    def norm(mb):
        values = xin[mb].astype(F32)
        inv_rms = lax.rsqrt(jnp.mean(values * values, axis=-1, keepdims=True) + NORM_EPSILON)
        return values, inv_rms

    def forward(mb, _):
        job = mb

        @pl.when(section == 0)
        def _():
            xin[mb] = inp[mb]

        @pl.when(section > 0)
        def _():
            forward_in(mb).wait_recv()

        values, inv_rms = norm(mb)
        gather(job, values * inv_rms * gain)
        for copy in keep(job):
            copy.start()

        @pl.when(mb == 0)
        def _():
            load_up.wait()
            load_down.wait()

        for h, acc in ((0, ya), (1, yb)):
            acc[...] = jnp.zeros_like(acc)

            @pl.loop(0, half // K_TILE)
            def _(t):
                cols = pl.ds(pl.multiple_of(t * K_TILE, K_TILE), K_TILE)
                depth = pl.ds(pl.multiple_of(h * half + t * K_TILE, K_TILE), K_TILE)
                acc[...] += jnp.dot(gath[job, h, :, cols], w_up[depth, :], preferred_element_type=F32)

        permuted(ya, yb, True)
        up = ya[...]
        up_keep[mb] = up
        hidden = up / (1.0 + jnp.exp(-up))
        ya[...] = hidden
        permuted(yb, ya, False)
        hid_rows = pl.ds(pl.multiple_of(mb * 128, 128), 128)
        for h, acc in ((0, ya), (1, yb)):
            hid_out[h, hid_rows, :] = acc[...].astype(BF16)

            @pl.loop(0, half // N_TILE)
            def _(t):
                cols = pl.ds(pl.multiple_of(t * N_TILE, N_TILE), N_TILE)
                wide = pl.ds(pl.multiple_of(h * half + t * N_TILE, N_TILE), N_TILE)
                part[h, :, cols] = jnp.dot(
                    hid_out[h, hid_rows, :], w_down[:, wide], preferred_element_type=F32
                ).astype(BF16)

        mixed = scatter(job)
        outs[mb] = (xin[mb].astype(F32) + mixed).astype(BF16)

        @pl.when(section < sections - 1)
        def _():
            forward_in(mb).start()

        return 0

    def backward(mb, _):
        job = micro + mb

        @pl.when(section == sections - 1)
        def _():
            gin[mb] = cot[mb]

        @pl.when(section < sections - 1)
        def _():
            backward_in(mb).wait_recv()

        gather(job, gin[mb].astype(F32))
        for copy in keep(job):
            copy.start()
        for h, acc in ((0, ya), (1, yb)):
            acc[...] = jnp.zeros_like(acc)

            @pl.loop(0, half // K_TILE)
            def _(t):
                cols = pl.ds(pl.multiple_of(t * K_TILE, K_TILE), K_TILE)
                wide = pl.ds(pl.multiple_of(h * half + t * K_TILE, K_TILE), K_TILE)
                acc[...] += lax.dot_general(gath[job, h, :, cols], w_down[:, wide], NT, preferred_element_type=F32)

        permuted(ya, yb, True)
        up = up_keep[mb]
        q = 1.0 / (1.0 + jnp.exp(-up))
        ya[...] = ya[...] * q * (1.0 + up * (1.0 - q))
        permuted(yb, ya, False)
        ug_rows = pl.ds(pl.multiple_of(mb * 128, 128), 128)
        for h, acc in ((0, ya), (1, yb)):
            ug_out[h, ug_rows, :] = acc[...].astype(BF16)

            @pl.loop(0, half // N_TILE)
            def _(t):
                cols = pl.ds(pl.multiple_of(t * N_TILE, N_TILE), N_TILE)
                depth = pl.ds(pl.multiple_of(h * half + t * N_TILE, N_TILE), N_TILE)
                part[h, :, cols] = lax.dot_general(
                    ug_out[h, ug_rows, :], w_up[depth, :], NT, preferred_element_type=F32
                ).astype(BF16)

        scaled = scatter(job) * gain
        values, inv_rms = norm(mb)
        term = inv_rms * scaled - values * (inv_rms * inv_rms * inv_rms) * jnp.mean(
            scaled * values, axis=-1, keepdims=True
        )
        grads[mb] = (gin[mb].astype(F32) + term).astype(BF16)

        @pl.when(section > 0)
        def _():
            backward_in(mb).start()

        return 0

    lax.fori_loop(0, micro, forward, 0)
    lax.fori_loop(0, micro, backward, 0)

    for job in range(2 * micro):
        for copy in keep(job):
            copy.wait()

    @pl.when(section < sections - 1)
    def _():
        for mb in range(micro):
            forward_in(mb).wait_send()

    @pl.when(section > 0)
    def _():
        for mb in range(micro):
            backward_in(mb).wait_send()


def layers(inputs, cotangent, gain, w_up, w_down):
    micro, toks, features = inputs.shape
    half, units, slab, jobs = features // 2, w_up.shape[1], SIDE * toks, 2 * micro
    tokens = slab * SIDE * CORES
    vmem = pl.BlockSpec(memory_space=pltpu.VMEM)
    hbm = pl.BlockSpec(memory_space=pl.ANY)
    dma = pltpu.SemaphoreType.DMA
    small = jax.ShapeDtypeStruct(inputs.shape, BF16)
    narrow = jax.ShapeDtypeStruct((2, micro * tokens, units), BF16)
    return pl.pallas_call(
        layers_kernel,
        out_shape=(
            small,
            small,
            jax.ShapeDtypeStruct((2, 2, micro * tokens, half), BF16),
            narrow,
            narrow,
        ),
        in_specs=[vmem, vmem, vmem, hbm, hbm],
        out_specs=(vmem, vmem, hbm, vmem, vmem),
        scratch_shapes=[
            pltpu.VMEM(w_up.shape, BF16),
            pltpu.VMEM(w_down.shape, BF16),
            pltpu.VMEM(inputs.shape, BF16),
            pltpu.VMEM(inputs.shape, BF16),
            pltpu.VMEM((jobs, 2, SIDE, toks, half), BF16),
            pltpu.VMEM((jobs, 2, tokens, half), BF16),
            pltpu.VMEM((2, tokens, half), BF16),
            pltpu.VMEM((jobs, 2, SIDE, slab, half), BF16),
            pltpu.VMEM((2, SIDE - 1, slab, half), BF16),
            pltpu.VMEM((jobs, 2, SIDE - 1, slab, half), BF16),
            pltpu.VMEM((2, SIDE, toks, half), BF16),
            pltpu.VMEM((jobs, 2, SIDE - 1, toks, half), BF16),
            pltpu.VMEM((tokens, units), F32),
            pltpu.VMEM((tokens, units), F32),
            pltpu.VMEM((micro, tokens, units), F32),
            pltpu.VMEM((2, slab, half), F32),
            dma((2,)),
            dma((jobs, 2)),
            dma((2, micro)),
            dma((2, micro)),
            dma((jobs, 2, SIDE - 1)),
            dma((jobs, 2, SIDE - 1)),
            dma((jobs, 2, SIDE - 1)),
            dma((jobs, 2, SIDE - 1)),
            dma((jobs, 2, SIDE)),
            dma((jobs, 2, SIDE)),
            dma((jobs, 2, SIDE)),
            dma((jobs, 2, SIDE)),
            dma((jobs, 2, SIDE - 1)),
            dma((jobs, 2, SIDE - 1)),
            dma((jobs, 2, SIDE - 1)),
            dma((jobs, 2, SIDE - 1)),
        ],
        compiler_params=pltpu.CompilerParams(
            collective_id=0, has_side_effects=True, vmem_limit_bytes=58 << 20
        ),
    )(inputs, cotangent, gain, w_up, w_down)


def shards(
    inputs, cotangent, gains, up_blocks, up_index, up_count, down_blocks, down_index, down_count
):
    features = inputs.shape[2]
    row_blocks = features // BLOCK
    group_blocks = FF // lax.axis_size("tp") // BLOCK
    w_up = densify(up_blocks[0].reshape(-1, BLOCK, BLOCK), up_index[0], up_count[0, 0], row_blocks, group_blocks)
    w_down = densify(
        down_blocks[0].reshape(-1, BLOCK, BLOCK), down_index[0], down_count[0, 0], group_blocks, row_blocks
    )
    outs, grads, rows, hidden, up_grad = layers(inputs, cotangent, gains, w_up, w_down)
    up_grads = weight_grad(rows[0], up_grad, up_index[0], up_count[0], True, group_blocks)
    down_grads = weight_grad(hidden, rows[1], down_index[0], down_count[0], False, row_blocks)
    return (
        outs[None],
        grads[None],
        up_grads.reshape(1, -1, BLOCK * BLOCK),
        down_grads.reshape(1, -1, BLOCK * BLOCK),
    )


def solution(mesh):
    return jax.shard_map(
        shards,
        mesh=mesh,
        in_specs=(
            P(None, "tp", None),
            P(None, "tp", None),
            P("section", None),
            P("section", "tp", None),
            P("section", "tp"),
            P("section", "tp"),
            P("section", "tp", None),
            P("section", "tp"),
            P("section", "tp"),
        ),
        out_specs=(
            P("section", None, "tp", None),
            P("section", None, "tp", None),
            P("section", "tp", None),
            P("section", "tp", None),
        ),
        check_vma=False,
    )
```

```python
import functools

import jax
import jax.numpy as jnp
from jax import lax
from jax.experimental import pallas as pl
from jax.experimental.pallas import tpu as pltpu
from jax.sharding import PartitionSpec as P

FF = 16384
BLOCK = 64
NORM_EPSILON = 1e-05
MESH = pl.DeviceIdType.MESH
F32 = jnp.float32
BF16 = jnp.bfloat16
SIDE = 4
CORES = 2


LINES = BLOCK * BLOCK // 128
GROUP = 16
VMEM_LIMIT = 60 << 20


def low_half(shape):
    return lax.broadcasted_iota(jnp.int32, shape, 1) < BLOCK


def place_kernel(slots_ref, blocks_ref, out_ref, lines, mixed, *, row_major, row_blocks, col_blocks):
    step = pl.program_id(0)

    @pl.when(step == 0)
    def _():
        @pl.loop(0, blocks_ref.shape[0] // GROUP)
        def _(g):
            rows = pl.ds(pl.multiple_of(g * GROUP, GROUP), GROUP)
            for k in range(LINES):
                lines[pl.ds(pl.multiple_of((g * LINES + k) * GROUP, GROUP), GROUP), :] = blocks_ref[
                    rows, 128 * k : 128 * (k + 1)
                ].astype(F32)

    low = low_half((LINES, 128))

    def block(place):
        slot = slots_ref[place]
        used = jnp.maximum(slot, 0)
        first = lax.div(used, GROUP) * (GROUP * LINES) + lax.rem(used, GROUP)
        value = lines[pl.ds(first, LINES, stride=GROUP), :]
        return jnp.where(slot >= 0, value, jnp.zeros_like(value))

    def pair(place, n):
        a, b = block(place), block(place + 1)
        mixed[pl.ds(n * BLOCK, LINES, stride=2), :] = jnp.where(low, a, pltpu.roll(b, BLOCK, 1))
        mixed[pl.ds(n * BLOCK + 1, LINES, stride=2), :] = jnp.where(low, pltpu.roll(a, BLOCK, 1), b)
        return mixed[n * BLOCK : (n + 1) * BLOCK, :].astype(BF16)

    if row_major:
        rows = out_ref.shape[0] // BLOCK

        @pl.loop(0, rows)
        def _(row):
            for n in range(col_blocks // 2):
                out_ref[pl.ds(pl.multiple_of(row * BLOCK, BLOCK), BLOCK), n * 128 : (n + 1) * 128] = pair(
                    (step * rows + row) * col_blocks + 2 * n, n
                )
    else:
        cols = out_ref.shape[1] // 128

        @pl.loop(0, cols)
        def _(col):
            for n in range(row_blocks):
                out_ref[n * BLOCK : (n + 1) * BLOCK, pl.ds(pl.multiple_of(col * 128, 128), 128)] = pair(
                    n * col_blocks + (step * cols + col) * 2, n
                )


def densify(blocks, block_index, live_count, row_blocks, col_blocks):
    slot_count = blocks.shape[0]
    slots = jnp.arange(slot_count, dtype=jnp.int32)
    places = jnp.arange(row_blocks * col_blocks, dtype=jnp.int32)
    hit = (block_index[None, :] == places[:, None]) & (slots < live_count)[None, :]
    slot_of_place = jnp.max(jnp.where(hit, slots[None, :], -1), axis=1)
    row_major = row_blocks > col_blocks
    steps = 8
    rows, cols = row_blocks * BLOCK, col_blocks * BLOCK
    if row_major:
        out_spec = pl.BlockSpec((rows // steps, cols), lambda i, *_: (i, 0))
    else:
        out_spec = pl.BlockSpec((rows, cols // steps), lambda i, *_: (0, i))
    return pl.pallas_call(
        functools.partial(place_kernel, row_major=row_major, row_blocks=row_blocks, col_blocks=col_blocks),
        out_shape=jax.ShapeDtypeStruct((rows, cols), blocks.dtype),
        grid_spec=pltpu.PrefetchScalarGridSpec(
            num_scalar_prefetch=1,
            grid=(steps,),
            in_specs=[pl.BlockSpec(blocks.shape, lambda i, *_: (0, 0), pipeline_mode=pl.Buffered(1))],
            out_specs=out_spec,
            scratch_shapes=[
                pltpu.VMEM((slot_count * LINES, 128), F32),
                pltpu.VMEM((min(row_blocks, col_blocks) * BLOCK, 128), F32),
            ],
        ),
        compiler_params=pltpu.CompilerParams(vmem_limit_bytes=VMEM_LIMIT),
    )(slot_of_place, blocks)


def weight_grad_kernel(index_ref, count_ref, lhs_ref, rhs_ref, out_ref, dense, lines, *, up, col_blocks):
    step = pl.program_id(0)
    product = lax.dot_general(lhs_ref[0], rhs_ref[0], (((0,), (0,)), ((), ())), preferred_element_type=F32)
    height, width = product.shape
    chunks = width // 128
    column = height * pl.num_programs(0) if up else height
    for j in range(chunks):
        first = j * column + step * height if up else (step * chunks + j) * column
        dense[pl.ds(pl.multiple_of(first, 128), height), :] = product[:, 128 * j : 128 * (j + 1)]

    @pl.when(step == pl.num_programs(0) - 1)
    def _():
        count = count_ref[0]
        low = low_half((LINES, 128))

        @pl.loop(0, out_ref.shape[0] // GROUP)
        def _(g):
            for i in range(GROUP):
                slot = g * GROUP + i
                place = index_ref[slot]
                block_row, block_col = lax.div(place, col_blocks), lax.rem(place, col_blocks)
                first = lax.div(block_col, 2) * column + block_row * BLOCK
                odd = lax.rem(block_col, 2)
                even_rows = dense[pl.ds(first, LINES, stride=2), :]
                odd_rows = dense[pl.ds(first + 1, LINES, stride=2), :]
                value = jnp.where(
                    low,
                    jnp.where(odd == 1, pltpu.roll(even_rows, BLOCK, 1), even_rows),
                    jnp.where(odd == 1, odd_rows, pltpu.roll(odd_rows, BLOCK, 1)),
                )
                lines[pl.ds(i, LINES, stride=GROUP), :] = jnp.where(slot < count, value, jnp.zeros_like(value))
            rows = pl.ds(pl.multiple_of(g * GROUP, GROUP), GROUP)
            for k in range(LINES):
                out_ref[rows, 128 * k : 128 * (k + 1)] = lines[k * GROUP : (k + 1) * GROUP, :].astype(BF16)


def weight_grad(lhs, rhs, block_index, live_count, up, col_blocks):
    halves, tokens, width = (lhs if up else rhs).shape
    units = (rhs if up else lhs).shape[2]
    tile = 512
    per_half = width // tile
    wide = pl.BlockSpec((1, tokens, tile), lambda i, *_: (i // per_half, 0, i % per_half))
    narrow = pl.BlockSpec((1, tokens, units), lambda i, *_: (i // per_half, 0, 0))
    slots = block_index.shape[0]
    return pl.pallas_call(
        functools.partial(weight_grad_kernel, up=up, col_blocks=col_blocks),
        out_shape=jax.ShapeDtypeStruct((slots, BLOCK * BLOCK), BF16),
        grid_spec=pltpu.PrefetchScalarGridSpec(
            num_scalar_prefetch=2,
            grid=(halves * per_half,),
            in_specs=[wide, narrow] if up else [narrow, wide],
            out_specs=pl.BlockSpec((slots, BLOCK * BLOCK), lambda i, *_: (0, 0), pipeline_mode=pl.Buffered(1)),
            scratch_shapes=[
                pltpu.VMEM((units * halves * width // 128, 128), F32),
                pltpu.VMEM((LINES * GROUP, 128), F32),
            ],
        ),
        compiler_params=pltpu.CompilerParams(vmem_limit_bytes=VMEM_LIMIT),
    )(block_index, live_count, lhs, rhs)


def layers_kernel(
    inp, cot, gain_ref, w_up_hbm, w_down_hbm,
    outs, grads, normed_hbm, grad_hbm, hid_out, ug_out,
    w_up, w_down, xin, gin, ibuf, gath, part, xbuf, sbuf, obuf, rsend, rbuf, ya, yb, up_keep, tmp,
    w_sem, keep_sem, sec_send, sec_recv, p1_send, p1_recv, p2_send, p2_recv, sib_send, sib_recv,
    r0_send, r0_recv, r1_send, r1_recv, r2_send, r2_recv,
):
    micro, toks, features = inp.shape
    half = features // 2
    slab = SIDE * toks
    section, tp = lax.axis_index("section"), lax.axis_index("tp")
    sections = lax.axis_size("section")
    core = lax.rem(tp, CORES)
    y = lax.rem(lax.div(tp, CORES), SIDE)
    z = lax.div(tp, CORES * SIDE)
    sibling = {"tp": tp + 1 - 2 * core}
    inner = (z, y)
    outer = (y, z)

    def at(zz, yy):
        return {"tp": (zz * SIDE + yy) * CORES + core}

    def inner_peer(h, k):
        i = lax.rem(inner[h] + k, SIDE)
        return i, (at(i, y) if h == 0 else at(z, i))

    def outer_peer(h, k):
        o = lax.rem(outer[h] + k, SIDE)
        return o, (at(z, o) if h == 0 else at(o, y))

    def remote(src, dst, send, recv, device):
        return pltpu.make_async_remote_copy(
            src_ref=src, dst_ref=dst, send_sem=send, recv_sem=recv, device_id=device, device_id_type=MESH
        )

    load_up = pltpu.make_async_copy(w_up_hbm, w_up, w_sem.at[0])
    load_down = pltpu.make_async_copy(w_down_hbm, w_down, w_sem.at[1])
    load_up.start()
    load_down.start()

    barrier = pltpu.get_barrier_semaphore()
    peers = [sibling]
    for h in range(2):
        peers += [inner_peer(h, k)[1] for k in range(1, SIDE)]
    for peer in peers:
        pl.semaphore_signal(barrier, inc=1, device_id=peer, device_id_type=MESH)

    @pl.when(section > 0)
    def _():
        pl.semaphore_signal(barrier, inc=1, device_id={"section": section - 1}, device_id_type=MESH)

    @pl.when(section < sections - 1)
    def _():
        pl.semaphore_signal(barrier, inc=1, device_id={"section": section + 1}, device_id_type=MESH)

    @pl.when((section == 0) | (section == sections - 1))
    def _():
        pl.semaphore_wait(barrier, len(peers) + 1)

    @pl.when((section > 0) & (section < sections - 1))
    def _():
        pl.semaphore_wait(barrier, len(peers) + 2)

    ORDER = (1, 3, 2)

    def slab_rows(o, c):
        return pl.ds(pl.multiple_of((o * CORES + c) * slab, slab), slab)

    def gather(job, values):
        first = []
        for h in range(2):
            mine = ibuf.at[job, h, inner[h]]
            mine[...] = values[:, h * half : (h + 1) * half].astype(BF16)
        for k in ORDER:
            for h in range(2):
                mine = ibuf.at[job, h, inner[h]]
                copy = remote(mine, mine, p1_send.at[job, h, k - 1], p1_recv.at[job, h, k - 1], inner_peer(h, k)[1])
                copy.start()
                first.append(copy)
        for copy in first:
            copy.wait_recv()
        second, side = {}, []
        for h in range(2):
            for i in range(SIDE):
                tmp[h, i * toks : (i + 1) * toks, :] = ibuf[job, h, i].astype(F32)
            rows = slab_rows(outer[h], core)
            gath[job, h, rows, :] = tmp[h].astype(BF16)
            mine = gath.at[job, h, rows]
            for k in ORDER:
                copy = remote(mine, mine, p2_send.at[job, h, k - 1], p2_recv.at[job, h, k - 1], outer_peer(h, k)[1])
                copy.start()
                second[h, k] = copy
            copy = remote(mine, mine, sib_send.at[job, h, 0], sib_recv.at[job, h, 0], sibling)
            copy.start()
            side.append(copy)
        for k in ORDER:
            for h in range(2):
                second[h, k].wait_recv()
                came = gath.at[job, h, slab_rows(outer_peer(h, SIDE - k)[0], core)]
                copy = remote(came, came, sib_send.at[job, h, k], sib_recv.at[job, h, k], sibling)
                copy.start()
                side.append(copy)
        for copy in side:
            copy.wait_recv()
        for copy in first + list(second.values()) + side:
            copy.wait_send()

    def keep(job, mb, rows_hbm):
        return [
            pltpu.make_async_copy(
                gath.at[job, h],
                rows_hbm.at[h, pl.ds(pl.multiple_of(mb * 128, 128), 128)],
                keep_sem.at[job, h],
            )
            for h in range(2)
        ]

    def permuted(target, source, add):
        for a in range(SIDE):
            for c in range(CORES):
                for b in range(SIDE):
                    to, of = ((a * CORES + c) * SIDE + b) * toks, ((b * CORES + c) * SIDE + a) * toks
                    moved = source[of : of + toks, :]
                    target[to : to + toks, :] = target[to : to + toks, :] + moved if add else moved

    def scatter(job):
        sends = []
        zero = []
        for h in range(2):
            for o in range(SIDE):
                copy = remote(
                    part.at[h, slab_rows(o, 1 - core)],
                    xbuf.at[job, h, o],
                    r0_send.at[job, h, o],
                    r0_recv.at[job, h, o],
                    sibling,
                )
                copy.start()
                zero.append(copy)
        one = {}
        for copy in zero:
            copy.wait_recv()
        for h in range(2):
            for k in ORDER + (0,):
                o, peer = outer_peer(h, k)
                both = part[h, slab_rows(o, core), :].astype(F32) + xbuf[job, h, o].astype(F32)
                if k:
                    sbuf[h, k - 1] = both.astype(BF16)
                    copy = remote(
                        sbuf.at[h, k - 1],
                        obuf.at[job, h, k - 1],
                        r1_send.at[job, h, k - 1],
                        r1_recv.at[job, h, k - 1],
                        peer,
                    )
                    copy.start()
                    one[h, k] = copy
                else:
                    tmp[h] = both
        two = {}
        for h in range(2):
            for k in ORDER:
                one[h, k].wait_recv()
            tmp[h] = tmp[h] + (obuf[job, h, 0].astype(F32) + obuf[job, h, 1].astype(F32) + obuf[job, h, 2].astype(F32))
            for i in range(SIDE):
                rsend[h, i] = tmp[h, i * toks : (i + 1) * toks, :].astype(BF16)
            for k in ORDER:
                i, peer = inner_peer(h, k)
                copy = remote(
                    rsend.at[h, i],
                    rbuf.at[job, h, k - 1],
                    r2_send.at[job, h, k - 1],
                    r2_recv.at[job, h, k - 1],
                    peer,
                )
                copy.start()
                two[h, k] = copy
        sums = []
        for h in range(2):
            for k in ORDER:
                two[h, k].wait_recv()
            own = rsend[h, inner[h]].astype(F32)
            sums.append(
                own + (rbuf[job, h, 0].astype(F32) + rbuf[job, h, 1].astype(F32) + rbuf[job, h, 2].astype(F32))
            )
        for copy in zero + list(one.values()) + list(two.values()):
            copy.wait_send()
        return jnp.concatenate(sums, axis=1)

    gain = gain_ref[...].astype(F32)
    K_TILE = 1024
    N_TILE = 512
    NT = (((1,), (1,)), ((), ()))

    def forward_in(mb):
        return remote(outs.at[mb], xin.at[mb], sec_send.at[0, mb], sec_recv.at[0, mb], {"section": section + 1})

    def backward_in(mb):
        return remote(grads.at[mb], gin.at[mb], sec_send.at[1, mb], sec_recv.at[1, mb], {"section": section - 1})

    def norm(mb):
        values = xin[mb].astype(F32)
        inv_rms = lax.rsqrt(jnp.mean(values * values, axis=-1, keepdims=True) + NORM_EPSILON)
        return values, inv_rms

    def forward(mb, _):
        job = mb

        @pl.when(section == 0)
        def _():
            xin[mb] = inp[mb]

        @pl.when(section > 0)
        def _():
            forward_in(mb).wait_recv()

        values, inv_rms = norm(mb)
        gather(job, values * inv_rms * gain)
        for copy in keep(job, mb, normed_hbm):
            copy.start()

        @pl.when(mb == 0)
        def _():
            load_up.wait()
            load_down.wait()

        for h, acc in ((0, ya), (1, yb)):
            acc[...] = jnp.zeros_like(acc)

            @pl.loop(0, half // K_TILE)
            def _(t):
                cols = pl.ds(pl.multiple_of(t * K_TILE, K_TILE), K_TILE)
                depth = pl.ds(pl.multiple_of(h * half + t * K_TILE, K_TILE), K_TILE)
                acc[...] += jnp.dot(gath[job, h, :, cols], w_up[depth, :], preferred_element_type=F32)

        permuted(ya, yb, True)
        up = ya[...]
        up_keep[mb] = up
        hidden = up / (1.0 + jnp.exp(-up))
        ya[...] = hidden
        permuted(yb, ya, False)
        hid_rows = pl.ds(pl.multiple_of(mb * 128, 128), 128)
        for h, acc in ((0, ya), (1, yb)):
            hid_out[h, hid_rows, :] = acc[...].astype(BF16)

            @pl.loop(0, half // N_TILE)
            def _(t):
                cols = pl.ds(pl.multiple_of(t * N_TILE, N_TILE), N_TILE)
                wide = pl.ds(pl.multiple_of(h * half + t * N_TILE, N_TILE), N_TILE)
                part[h, :, cols] = jnp.dot(
                    hid_out[h, hid_rows, :], w_down[:, wide], preferred_element_type=F32
                ).astype(BF16)

        mixed = scatter(job)
        outs[mb] = (xin[mb].astype(F32) + mixed).astype(BF16)

        @pl.when(section < sections - 1)
        def _():
            forward_in(mb).start()

        return 0

    def backward(mb, _):
        job = micro + mb

        @pl.when(section == sections - 1)
        def _():
            gin[mb] = cot[mb]

        @pl.when(section < sections - 1)
        def _():
            backward_in(mb).wait_recv()

        gather(job, gin[mb].astype(F32))
        for copy in keep(job, mb, grad_hbm):
            copy.start()
        for h, acc in ((0, ya), (1, yb)):
            acc[...] = jnp.zeros_like(acc)

            @pl.loop(0, half // K_TILE)
            def _(t):
                cols = pl.ds(pl.multiple_of(t * K_TILE, K_TILE), K_TILE)
                wide = pl.ds(pl.multiple_of(h * half + t * K_TILE, K_TILE), K_TILE)
                acc[...] += lax.dot_general(gath[job, h, :, cols], w_down[:, wide], NT, preferred_element_type=F32)

        permuted(ya, yb, True)
        up = up_keep[mb]
        q = 1.0 / (1.0 + jnp.exp(-up))
        ya[...] = ya[...] * q * (1.0 + up * (1.0 - q))
        permuted(yb, ya, False)
        ug_rows = pl.ds(pl.multiple_of(mb * 128, 128), 128)
        for h, acc in ((0, ya), (1, yb)):
            ug_out[h, ug_rows, :] = acc[...].astype(BF16)

            @pl.loop(0, half // N_TILE)
            def _(t):
                cols = pl.ds(pl.multiple_of(t * N_TILE, N_TILE), N_TILE)
                depth = pl.ds(pl.multiple_of(h * half + t * N_TILE, N_TILE), N_TILE)
                part[h, :, cols] = lax.dot_general(
                    ug_out[h, ug_rows, :], w_up[depth, :], NT, preferred_element_type=F32
                ).astype(BF16)

        scaled = scatter(job) * gain
        values, inv_rms = norm(mb)
        term = inv_rms * scaled - values * (inv_rms * inv_rms * inv_rms) * jnp.mean(
            scaled * values, axis=-1, keepdims=True
        )
        grads[mb] = (gin[mb].astype(F32) + term).astype(BF16)

        @pl.when(section > 0)
        def _():
            backward_in(mb).start()

        return 0

    lax.fori_loop(0, micro, forward, 0)
    lax.fori_loop(0, micro, backward, 0)

    for mb in range(micro):
        for copy in keep(mb, mb, normed_hbm) + keep(micro + mb, mb, grad_hbm):
            copy.wait()

    @pl.when(section < sections - 1)
    def _():
        for mb in range(micro):
            forward_in(mb).wait_send()

    @pl.when(section > 0)
    def _():
        for mb in range(micro):
            backward_in(mb).wait_send()


def layers(inputs, cotangent, gain, w_up, w_down):
    micro, toks, features = inputs.shape
    half, units, slab, jobs = features // 2, w_up.shape[1], SIDE * toks, 2 * micro
    tokens = slab * SIDE * CORES
    vmem = pl.BlockSpec(memory_space=pltpu.VMEM)
    hbm = pl.BlockSpec(memory_space=pl.ANY)
    dma = pltpu.SemaphoreType.DMA
    small = jax.ShapeDtypeStruct(inputs.shape, BF16)
    wide = jax.ShapeDtypeStruct((2, micro * tokens, half), BF16)
    narrow = jax.ShapeDtypeStruct((2, micro * tokens, units), BF16)
    return pl.pallas_call(
        layers_kernel,
        out_shape=(
            small,
            small,
            wide,
            wide,
            narrow,
            narrow,
        ),
        in_specs=[vmem, vmem, vmem, hbm, hbm],
        out_specs=(vmem, vmem, hbm, hbm, vmem, vmem),
        scratch_shapes=[
            pltpu.VMEM(w_up.shape, BF16),
            pltpu.VMEM(w_down.shape, BF16),
            pltpu.VMEM(inputs.shape, BF16),
            pltpu.VMEM(inputs.shape, BF16),
            pltpu.VMEM((jobs, 2, SIDE, toks, half), BF16),
            pltpu.VMEM((jobs, 2, tokens, half), BF16),
            pltpu.VMEM((2, tokens, half), BF16),
            pltpu.VMEM((jobs, 2, SIDE, slab, half), BF16),
            pltpu.VMEM((2, SIDE - 1, slab, half), BF16),
            pltpu.VMEM((jobs, 2, SIDE - 1, slab, half), BF16),
            pltpu.VMEM((2, SIDE, toks, half), BF16),
            pltpu.VMEM((jobs, 2, SIDE - 1, toks, half), BF16),
            pltpu.VMEM((tokens, units), F32),
            pltpu.VMEM((tokens, units), F32),
            pltpu.VMEM((micro, tokens, units), F32),
            pltpu.VMEM((2, slab, half), F32),
            dma((2,)),
            dma((jobs, 2)),
            dma((2, micro)),
            dma((2, micro)),
            dma((jobs, 2, SIDE - 1)),
            dma((jobs, 2, SIDE - 1)),
            dma((jobs, 2, SIDE - 1)),
            dma((jobs, 2, SIDE - 1)),
            dma((jobs, 2, SIDE)),
            dma((jobs, 2, SIDE)),
            dma((jobs, 2, SIDE)),
            dma((jobs, 2, SIDE)),
            dma((jobs, 2, SIDE - 1)),
            dma((jobs, 2, SIDE - 1)),
            dma((jobs, 2, SIDE - 1)),
            dma((jobs, 2, SIDE - 1)),
        ],
        compiler_params=pltpu.CompilerParams(
            collective_id=0, has_side_effects=True, vmem_limit_bytes=58 << 20
        ),
    )(inputs, cotangent, gain, w_up, w_down)


def shards(
    inputs, cotangent, gains, up_blocks, up_index, up_count, down_blocks, down_index, down_count
):
    features = inputs.shape[2]
    row_blocks = features // BLOCK
    group_blocks = FF // lax.axis_size("tp") // BLOCK
    w_up = densify(up_blocks[0], up_index[0], up_count[0, 0], row_blocks, group_blocks)
    w_down = densify(down_blocks[0], down_index[0], down_count[0, 0], group_blocks, row_blocks)
    outs, grads, normed, grad_rows, hidden, up_grad = layers(inputs, cotangent, gains, w_up, w_down)
    up_grads = weight_grad(normed, up_grad, up_index[0], up_count[0], True, group_blocks)
    down_grads = weight_grad(hidden, grad_rows, down_index[0], down_count[0], False, row_blocks)
    return (
        outs[None],
        grads[None],
        up_grads[None],
        down_grads[None],
    )


def solution(mesh):
    return jax.shard_map(
        shards,
        mesh=mesh,
        in_specs=(
            P(None, "tp", None),
            P(None, "tp", None),
            P("section", None),
            P("section", "tp", None),
            P("section", "tp"),
            P("section", "tp"),
            P("section", "tp", None),
            P("section", "tp"),
            P("section", "tp"),
        ),
        out_specs=(
            P("section", None, "tp", None),
            P("section", None, "tp", None),
            P("section", "tp", None),
            P("section", "tp", None),
        ),
        check_vma=False,
    )
```

```python
import functools

import jax
import jax.numpy as jnp
from jax import lax
from jax.experimental import pallas as pl
from jax.experimental.pallas import tpu as pltpu
from jax.sharding import PartitionSpec as P

FF = 16384
BLOCK = 64
NORM_EPSILON = 1e-05
MESH = pl.DeviceIdType.MESH
F32 = jnp.float32
BF16 = jnp.bfloat16
SIDE = 4
CORES = 2


LINES = BLOCK * BLOCK // 128
GROUP = 16
VMEM_LIMIT = 60 << 20


def low_half(shape):
    return lax.broadcasted_iota(jnp.int32, shape, 1) < BLOCK


def place_kernel(slots_ref, blocks_ref, out_ref, lines, mixed, *, row_major, row_blocks, col_blocks):
    step = pl.program_id(0)

    @pl.when(step == 0)
    def _():
        @pl.loop(0, blocks_ref.shape[0] // GROUP)
        def _(g):
            rows = pl.ds(pl.multiple_of(g * GROUP, GROUP), GROUP)
            for k in range(LINES):
                lines[pl.ds(pl.multiple_of((g * LINES + k) * GROUP, GROUP), GROUP), :] = blocks_ref[
                    rows, 128 * k : 128 * (k + 1)
                ].astype(F32)

    low = low_half((LINES, 128))

    def block(place):
        slot = slots_ref[place]
        used = jnp.maximum(slot, 0)
        first = lax.div(used, GROUP) * (GROUP * LINES) + lax.rem(used, GROUP)
        value = lines[pl.ds(first, LINES, stride=GROUP), :]
        return jnp.where(slot >= 0, value, jnp.zeros_like(value))

    def pair(place, n):
        a, b = block(place), block(place + 1)
        mixed[pl.ds(n * BLOCK, LINES, stride=2), :] = jnp.where(low, a, pltpu.roll(b, BLOCK, 1))
        mixed[pl.ds(n * BLOCK + 1, LINES, stride=2), :] = jnp.where(low, pltpu.roll(a, BLOCK, 1), b)
        return mixed[n * BLOCK : (n + 1) * BLOCK, :].astype(BF16)

    if row_major:
        rows = out_ref.shape[0] // BLOCK

        @pl.loop(0, rows)
        def _(row):
            for n in range(col_blocks // 2):
                out_ref[pl.ds(pl.multiple_of(row * BLOCK, BLOCK), BLOCK), n * 128 : (n + 1) * 128] = pair(
                    (step * rows + row) * col_blocks + 2 * n, n
                )
    else:
        cols = out_ref.shape[1] // 128

        @pl.loop(0, cols)
        def _(col):
            for n in range(row_blocks):
                out_ref[n * BLOCK : (n + 1) * BLOCK, pl.ds(pl.multiple_of(col * 128, 128), 128)] = pair(
                    n * col_blocks + (step * cols + col) * 2, n
                )


def densify(blocks, block_index, live_count, row_blocks, col_blocks):
    slot_count = blocks.shape[0]
    slots = jnp.arange(slot_count, dtype=jnp.int32)
    places = jnp.arange(row_blocks * col_blocks, dtype=jnp.int32)
    hit = (block_index[None, :] == places[:, None]) & (slots < live_count)[None, :]
    slot_of_place = jnp.max(jnp.where(hit, slots[None, :], -1), axis=1)
    row_major = row_blocks > col_blocks
    steps = 8
    rows, cols = row_blocks * BLOCK, col_blocks * BLOCK
    if row_major:
        out_spec = pl.BlockSpec((rows // steps, cols), lambda i, *_: (i, 0))
    else:
        out_spec = pl.BlockSpec((rows, cols // steps), lambda i, *_: (0, i))
    return pl.pallas_call(
        functools.partial(place_kernel, row_major=row_major, row_blocks=row_blocks, col_blocks=col_blocks),
        out_shape=jax.ShapeDtypeStruct((rows, cols), blocks.dtype),
        grid_spec=pltpu.PrefetchScalarGridSpec(
            num_scalar_prefetch=1,
            grid=(steps,),
            in_specs=[pl.BlockSpec(blocks.shape, lambda i, *_: (0, 0), pipeline_mode=pl.Buffered(1))],
            out_specs=out_spec,
            scratch_shapes=[
                pltpu.VMEM((slot_count * LINES, 128), F32),
                pltpu.VMEM((min(row_blocks, col_blocks) * BLOCK, 128), F32),
            ],
        ),
        compiler_params=pltpu.CompilerParams(vmem_limit_bytes=VMEM_LIMIT),
    )(slot_of_place, blocks)


def weight_grad_kernel(index_ref, count_ref, lhs_ref, rhs_ref, out_ref, dense, lines, *, up, col_blocks):
    step = pl.program_id(0)
    product = lax.dot_general(lhs_ref[0], rhs_ref[0], (((0,), (0,)), ((), ())), preferred_element_type=F32)
    height, width = product.shape
    chunks = width // 128
    column = height * pl.num_programs(0) if up else height
    for j in range(chunks):
        first = j * column + step * height if up else (step * chunks + j) * column
        dense[pl.ds(pl.multiple_of(first, 128), height), :] = product[:, 128 * j : 128 * (j + 1)]

    @pl.when(step == pl.num_programs(0) - 1)
    def _():
        count = count_ref[0]
        low = low_half((LINES, 128))

        @pl.loop(0, out_ref.shape[0] // GROUP)
        def _(g):
            for i in range(GROUP):
                slot = g * GROUP + i
                place = index_ref[slot]
                block_row, block_col = lax.div(place, col_blocks), lax.rem(place, col_blocks)
                first = lax.div(block_col, 2) * column + block_row * BLOCK
                odd = lax.rem(block_col, 2)
                even_rows = dense[pl.ds(first, LINES, stride=2), :]
                odd_rows = dense[pl.ds(first + 1, LINES, stride=2), :]
                value = jnp.where(
                    low,
                    jnp.where(odd == 1, pltpu.roll(even_rows, BLOCK, 1), even_rows),
                    jnp.where(odd == 1, odd_rows, pltpu.roll(odd_rows, BLOCK, 1)),
                )
                lines[pl.ds(i, LINES, stride=GROUP), :] = jnp.where(slot < count, value, jnp.zeros_like(value))
            rows = pl.ds(pl.multiple_of(g * GROUP, GROUP), GROUP)
            for k in range(LINES):
                out_ref[rows, 128 * k : 128 * (k + 1)] = lines[k * GROUP : (k + 1) * GROUP, :].astype(BF16)


def weight_grad(lhs, rhs, block_index, live_count, up, col_blocks):
    halves, tokens, width = (lhs if up else rhs).shape
    units = (rhs if up else lhs).shape[2]
    tile = 512
    per_half = width // tile
    wide = pl.BlockSpec((1, tokens, tile), lambda i, *_: (i // per_half, 0, i % per_half))
    narrow = pl.BlockSpec((1, tokens, units), lambda i, *_: (i // per_half, 0, 0))
    slots = block_index.shape[0]
    return pl.pallas_call(
        functools.partial(weight_grad_kernel, up=up, col_blocks=col_blocks),
        out_shape=jax.ShapeDtypeStruct((slots, BLOCK * BLOCK), BF16),
        grid_spec=pltpu.PrefetchScalarGridSpec(
            num_scalar_prefetch=2,
            grid=(halves * per_half,),
            in_specs=[wide, narrow] if up else [narrow, wide],
            out_specs=pl.BlockSpec((slots, BLOCK * BLOCK), lambda i, *_: (0, 0), pipeline_mode=pl.Buffered(1)),
            scratch_shapes=[
                pltpu.VMEM((units * halves * width // 128, 128), F32),
                pltpu.VMEM((LINES * GROUP, 128), F32),
            ],
        ),
        compiler_params=pltpu.CompilerParams(vmem_limit_bytes=VMEM_LIMIT),
    )(block_index, live_count, lhs, rhs)


CHUNKS = 2


def layers_kernel(
    inp, cot, gain_ref, w_up_hbm, w_down_hbm,
    outs, grads, normed_hbm, grad_hbm, hid_out, ug_out,
    w_up, w_down, xin, gin, ibuf, gath, part, xbuf, sbuf, obuf, rsend, rbuf, ya, yb, up_keep, tmp,
    w_sem, keep_sem, sec_send, sec_recv, p1_send, p1_recv, p2_send, p2_recv, sib_send, sib_recv,
    r0_send, r0_recv, r1_send, r1_recv, r2_send, r2_recv,
):
    micro, toks, features = inp.shape
    half = features // 2
    width = half // CHUNKS
    slab = SIDE * toks
    core_rows = SIDE * slab
    tokens = CORES * core_rows
    section, tp = lax.axis_index("section"), lax.axis_index("tp")
    sections = lax.axis_size("section")
    core = lax.rem(tp, CORES)
    y = lax.rem(lax.div(tp, CORES), SIDE)
    z = lax.div(tp, CORES * SIDE)
    sibling = {"tp": tp + 1 - 2 * core}
    inner = (z, y)
    outer = (y, z)
    SENDING, WAITING = (2, 1, 3), (1, 3, 2)

    def at(zz, yy):
        return {"tp": (zz * SIDE + yy) * CORES + core}

    def inner_peer(h, k):
        i = lax.rem(inner[h] + k, SIDE)
        return i, (at(i, y) if h == 0 else at(z, i))

    def outer_peer(h, k):
        o = lax.rem(outer[h] + k, SIDE)
        return o, (at(z, o) if h == 0 else at(o, y))

    def remote(src, dst, send, recv, device):
        return pltpu.make_async_remote_copy(
            src_ref=src, dst_ref=dst, send_sem=send, recv_sem=recv, device_id=device, device_id_type=MESH
        )

    load_up = pltpu.make_async_copy(w_up_hbm, w_up, w_sem.at[0])
    load_down = pltpu.make_async_copy(w_down_hbm, w_down, w_sem.at[1])
    load_up.start()
    load_down.start()

    barrier = pltpu.get_barrier_semaphore()
    peers = [sibling]
    for h in range(2):
        peers += [inner_peer(h, k)[1] for k in range(1, SIDE)]
    for peer in peers:
        pl.semaphore_signal(barrier, inc=1, device_id=peer, device_id_type=MESH)

    @pl.when(section > 0)
    def _():
        pl.semaphore_signal(barrier, inc=1, device_id={"section": section - 1}, device_id_type=MESH)

    @pl.when(section < sections - 1)
    def _():
        pl.semaphore_signal(barrier, inc=1, device_id={"section": section + 1}, device_id_type=MESH)

    @pl.when((section == 0) | (section == sections - 1))
    def _():
        pl.semaphore_wait(barrier, len(peers) + 1)

    @pl.when((section > 0) & (section < sections - 1))
    def _():
        pl.semaphore_wait(barrier, len(peers) + 2)

    def core_slabs(c):
        return pl.ds(pl.multiple_of(c * core_rows, core_rows), core_rows)

    def slab_rows(o, c):
        return pl.ds(pl.multiple_of((c * SIDE + o) * slab, slab), slab)

    def first_copies(job, h):
        ref = ibuf.at[job, h, pl.ds(0, SIDE - 1)]
        return remote(ref, ref, p1_send.at[job, h], p1_recv.at[job, h], sibling)

    def second_sends(job, h):
        ref = gath.at[job, h, pl.ds(0, (SIDE - 1) * slab)]
        return remote(ref, ref, p2_send.at[job, h], p2_recv.at[job, h, 0], sibling)

    def sibling_copies(job, h):
        ref = gath.at[job, h, core_slabs(1 - core)]
        return remote(ref, ref, sib_send.at[job, h], sib_recv.at[job, h], sibling)

    def exchange(job, h, q):
        return remote(
            part.at[h, q, core_slabs(1 - core)],
            xbuf.at[job, h, q],
            r0_send.at[job, h, q],
            r0_recv.at[job, h, q],
            sibling,
        )

    def outer_copies(job, h, q):
        ref = obuf.at[job, h, q]
        return remote(ref, ref, r1_send.at[job, h, q], r1_recv.at[job, h, q], sibling)

    def inner_copies(job, h):
        ref = rbuf.at[job, h]
        return remote(ref, ref, r2_send.at[job, h], r2_recv.at[job, h], sibling)

    def gather(job, values):
        for h in range(2):
            mine = ibuf.at[job, h, inner[h]]
            mine[...] = values[:, h * half : (h + 1) * half].astype(BF16)
            for k in SENDING:
                remote(mine, mine, p1_send.at[job, h], p1_recv.at[job, h], inner_peer(h, k)[1]).start()
        second = {}
        for h in range(2):
            first_copies(job, h).wait_recv()
            for i in range(SIDE):
                tmp[h, i * toks : (i + 1) * toks, :] = ibuf[job, h, i].astype(F32)
            rows = slab_rows(outer[h], core)
            gath[job, h, rows, :] = tmp[h].astype(BF16)
            mine = gath.at[job, h, rows]
            for k in SENDING:
                copy = remote(mine, mine, p2_send.at[job, h], p2_recv.at[job, h, k - 1], outer_peer(h, k)[1])
                copy.start()
                second[h, k] = copy
            remote(mine, mine, sib_send.at[job, h], sib_recv.at[job, h], sibling).start()
        for k in WAITING:
            for h in range(2):
                second[h, k].wait_recv()
                came = gath.at[job, h, slab_rows(outer_peer(h, SIDE - k)[0], core)]
                remote(came, came, sib_send.at[job, h], sib_recv.at[job, h], sibling).start()

    def keep(job, mb, rows_hbm):
        return [
            pltpu.make_async_copy(
                gath.at[job, h],
                rows_hbm.at[h, pl.ds(pl.multiple_of(mb * tokens, tokens), tokens)],
                keep_sem.at[job, h],
            )
            for h in range(2)
        ]

    def permuted(target, source, add):
        for c in range(CORES):
            for a in range(SIDE):
                for b in range(SIDE):
                    to, of = ((c * SIDE + a) * SIDE + b) * toks, ((c * SIDE + b) * SIDE + a) * toks
                    moved = source[of : of + toks, :]
                    target[to : to + toks, :] = target[to : to + toks, :] + moved if add else moved

    def scatter(job, product):
        def spread(h, q):
            exchange(job, h, q).wait_recv()
            sbuf[job, h, q] = part[h, q, core_slabs(core), :] + xbuf[job, h, q]
            for k in SENDING:
                o, peer = outer_peer(h, k)
                remote(
                    sbuf.at[job, h, q, pl.ds(pl.multiple_of(o * slab, slab), slab)],
                    obuf.at[job, h, q, k - 1],
                    r1_send.at[job, h, q],
                    r1_recv.at[job, h, q],
                    peer,
                ).start()

        steps = [(h, q) for q in range(CHUNKS) for h in range(2)]
        for n, (h, q) in enumerate(steps):
            part[h, q] = product(h, q).astype(BF16)
            exchange(job, h, q).start()
            if n:
                spread(*steps[n - 1])
        spread(*steps[-1])
        for h in range(2):
            for q in range(CHUNKS):
                outer_copies(job, h, q).wait_recv()
                own = sbuf[job, h, q, pl.ds(pl.multiple_of(outer[h] * slab, slab), slab), :].astype(F32)
                came = [obuf[job, h, q, k].astype(F32) for k in range(SIDE - 1)]
                tmp[h, :, q * width : (q + 1) * width] = own + (came[0] + came[1] + came[2])
            for i in range(SIDE):
                rsend[job, h, i] = tmp[h, i * toks : (i + 1) * toks, :].astype(BF16)
            for k in SENDING:
                i, peer = inner_peer(h, k)
                remote(
                    rsend.at[job, h, i], rbuf.at[job, h, k - 1], r2_send.at[job, h], r2_recv.at[job, h], peer
                ).start()
        for h, q in steps:
            exchange(job, h, q).wait_send()
        sums = []
        for h in range(2):
            inner_copies(job, h).wait_recv()
            came = [rbuf[job, h, k].astype(F32) for k in range(SIDE - 1)]
            sums.append(rsend[job, h, inner[h]].astype(F32) + (came[0] + came[1] + came[2]))
        return jnp.concatenate(sums, axis=1)

    gain = gain_ref[...].astype(F32)
    NT = (((1,), (1,)), ((), ()))

    def columns(h, q=0, size=half):
        return slice(h * half + q * size, h * half + (q + 1) * size)

    def forward_in(mb):
        return remote(outs.at[mb], xin.at[mb], sec_send.at[0, mb], sec_recv.at[0, mb], {"section": section + 1})

    def backward_in(mb):
        return remote(grads.at[mb], gin.at[mb], sec_send.at[1, mb], sec_recv.at[1, mb], {"section": section - 1})

    def norm(mb):
        values = xin[mb].astype(F32)
        inv_rms = lax.rsqrt(jnp.mean(values * values, axis=-1, keepdims=True) + NORM_EPSILON)
        return values, inv_rms

    def forward(mb, _):
        job = mb

        @pl.when(section == 0)
        def _():
            xin[mb] = inp[mb]

        @pl.when(section > 0)
        def _():
            forward_in(mb).wait_recv()

        values, inv_rms = norm(mb)
        gather(job, values * inv_rms * gain)

        @pl.when(mb == 0)
        def _():
            load_up.wait()
            load_down.wait()

        for h, acc in ((0, ya), (1, yb)):
            sibling_copies(job, h).wait_recv()
            acc[...] = jnp.dot(gath[job, h], w_up[columns(h), :], preferred_element_type=F32)

        permuted(ya, yb, True)
        up = ya[...]
        up_keep[mb] = up
        hidden = up / (1.0 + jnp.exp(-up))
        ya[...] = hidden
        permuted(yb, ya, False)
        kept = pl.ds(pl.multiple_of(mb * tokens, tokens), tokens)
        for h, acc in ((0, ya), (1, yb)):
            hid_out[h, kept, :] = acc[...].astype(BF16)

        def product(h, q):
            return jnp.dot(hid_out[h, kept, :], w_down[:, columns(h, q, width)], preferred_element_type=F32)

        mixed = scatter(job, product)
        outs[mb] = (xin[mb].astype(F32) + mixed).astype(BF16)

        @pl.when(section < sections - 1)
        def _():
            forward_in(mb).start()

        for copy in keep(job, mb, normed_hbm):
            copy.start()
        return 0

    def backward(mb, _):
        job = micro + mb

        @pl.when(section == sections - 1)
        def _():
            gin[mb] = cot[mb]

        @pl.when(section < sections - 1)
        def _():
            backward_in(mb).wait_recv()

        gather(job, gin[mb].astype(F32))
        for h, acc in ((0, ya), (1, yb)):
            sibling_copies(job, h).wait_recv()
            acc[...] = lax.dot_general(gath[job, h], w_down[:, columns(h)], NT, preferred_element_type=F32)
        for copy in keep(job, mb, grad_hbm):
            copy.start()

        permuted(ya, yb, True)
        up = up_keep[mb]
        q = 1.0 / (1.0 + jnp.exp(-up))
        ya[...] = ya[...] * q * (1.0 + up * (1.0 - q))
        permuted(yb, ya, False)
        kept = pl.ds(pl.multiple_of(mb * tokens, tokens), tokens)
        for h, acc in ((0, ya), (1, yb)):
            ug_out[h, kept, :] = acc[...].astype(BF16)

        def product(h, q):
            return lax.dot_general(ug_out[h, kept, :], w_up[columns(h, q, width), :], NT, preferred_element_type=F32)

        scaled = scatter(job, product) * gain
        values, inv_rms = norm(mb)
        term = inv_rms * scaled - values * (inv_rms * inv_rms * inv_rms) * jnp.mean(
            scaled * values, axis=-1, keepdims=True
        )
        grads[mb] = (gin[mb].astype(F32) + term).astype(BF16)

        @pl.when(section > 0)
        def _():
            backward_in(mb).start()

        return 0

    lax.fori_loop(0, micro, forward, 0)
    lax.fori_loop(0, micro, backward, 0)

    for mb in range(micro):
        for copy in keep(mb, mb, normed_hbm) + keep(micro + mb, mb, grad_hbm):
            copy.wait()
    for job in range(2 * micro):
        for h in range(2):
            for copies in (first_copies, second_sends, sibling_copies, inner_copies):
                copies(job, h).wait_send()
            for q in range(CHUNKS):
                outer_copies(job, h, q).wait_send()

    @pl.when(section < sections - 1)
    def _():
        for mb in range(micro):
            forward_in(mb).wait_send()

    @pl.when(section > 0)
    def _():
        for mb in range(micro):
            backward_in(mb).wait_send()


def layers(inputs, cotangent, gain, w_up, w_down):
    micro, toks, features = inputs.shape
    half, units, slab, jobs = features // 2, w_up.shape[1], SIDE * toks, 2 * micro
    core_rows, width = slab * SIDE, half // CHUNKS
    tokens = core_rows * CORES
    vmem = pl.BlockSpec(memory_space=pltpu.VMEM)
    hbm = pl.BlockSpec(memory_space=pl.ANY)
    dma = pltpu.SemaphoreType.DMA
    small = jax.ShapeDtypeStruct(inputs.shape, BF16)
    wide = jax.ShapeDtypeStruct((2, micro * tokens, half), BF16)
    narrow = jax.ShapeDtypeStruct((2, micro * tokens, units), BF16)
    return pl.pallas_call(
        layers_kernel,
        out_shape=(small, small, wide, wide, narrow, narrow),
        in_specs=[vmem, vmem, vmem, hbm, hbm],
        out_specs=(vmem, vmem, hbm, hbm, vmem, vmem),
        scratch_shapes=[
            pltpu.VMEM(w_up.shape, BF16),
            pltpu.VMEM(w_down.shape, BF16),
            pltpu.VMEM(inputs.shape, BF16),
            pltpu.VMEM(inputs.shape, BF16),
            pltpu.VMEM((jobs, 2, SIDE, toks, half), BF16),
            pltpu.VMEM((jobs, 2, tokens, half), BF16),
            pltpu.VMEM((2, CHUNKS, tokens, width), BF16),
            pltpu.VMEM((jobs, 2, CHUNKS, core_rows, width), BF16),
            pltpu.VMEM((jobs, 2, CHUNKS, core_rows, width), BF16),
            pltpu.VMEM((jobs, 2, CHUNKS, SIDE - 1, slab, width), BF16),
            pltpu.VMEM((jobs, 2, SIDE, toks, half), BF16),
            pltpu.VMEM((jobs, 2, SIDE - 1, toks, half), BF16),
            pltpu.VMEM((tokens, units), F32),
            pltpu.VMEM((tokens, units), F32),
            pltpu.VMEM((micro, tokens, units), F32),
            pltpu.VMEM((2, slab, half), F32),
            dma((2,)),
            dma((jobs, 2)),
            dma((2, micro)),
            dma((2, micro)),
            dma((jobs, 2)),
            dma((jobs, 2)),
            dma((jobs, 2)),
            dma((jobs, 2, SIDE - 1)),
            dma((jobs, 2)),
            dma((jobs, 2)),
            dma((jobs, 2, CHUNKS)),
            dma((jobs, 2, CHUNKS)),
            dma((jobs, 2, CHUNKS)),
            dma((jobs, 2, CHUNKS)),
            dma((jobs, 2)),
            dma((jobs, 2)),
        ],
        compiler_params=pltpu.CompilerParams(
            collective_id=0, has_side_effects=True, vmem_limit_bytes=VMEM_LIMIT
        ),
    )(inputs, cotangent, gain, w_up, w_down)


def shards(
    inputs, cotangent, gains, up_blocks, up_index, up_count, down_blocks, down_index, down_count
):
    features = inputs.shape[2]
    row_blocks = features // BLOCK
    group_blocks = FF // lax.axis_size("tp") // BLOCK
    w_up = densify(up_blocks[0], up_index[0], up_count[0, 0], row_blocks, group_blocks)
    w_down = densify(down_blocks[0], down_index[0], down_count[0, 0], group_blocks, row_blocks)
    outs, grads, normed, grad_rows, hidden, up_grad = layers(inputs, cotangent, gains, w_up, w_down)
    up_grads = weight_grad(normed, up_grad, up_index[0], up_count[0], True, group_blocks)
    down_grads = weight_grad(hidden, grad_rows, down_index[0], down_count[0], False, row_blocks)
    return (
        outs[None],
        grads[None],
        up_grads[None],
        down_grads[None],
    )


def solution(mesh):
    return jax.shard_map(
        shards,
        mesh=mesh,
        in_specs=(
            P(None, "tp", None),
            P(None, "tp", None),
            P("section", None),
            P("section", "tp", None),
            P("section", "tp"),
            P("section", "tp"),
            P("section", "tp", None),
            P("section", "tp"),
            P("section", "tp"),
        ),
        out_specs=(
            P("section", None, "tp", None),
            P("section", None, "tp", None),
            P("section", "tp", None),
            P("section", "tp", None),
        ),
        check_vma=False,
    )
```

```python
import functools

import jax
import jax.numpy as jnp
from jax import lax
from jax.experimental import pallas as pl
from jax.experimental.pallas import tpu as pltpu
from jax.sharding import PartitionSpec as P

FF = 16384
BLOCK = 64
NORM_EPSILON = 1e-05
MESH = pl.DeviceIdType.MESH
F32 = jnp.float32
BF16 = jnp.bfloat16
SIDE = 4
CORES = 2


LINES = BLOCK * BLOCK // 128
GROUP = 16
VMEM_LIMIT = 60 << 20
TILE = 2048
PAIRS = 32


def low_half(shape):
    return lax.broadcasted_iota(jnp.int32, shape, 1) < BLOCK


def place_kernel(slots_ref, blocks_ref, out_ref, lines, mixed, *, row_major, row_blocks, col_blocks):
    step = pl.program_id(0)

    @pl.when(step == 0)
    def _():
        @pl.loop(0, blocks_ref.shape[0] // (2 * GROUP))
        def _(t):
            for u in range(2):
                g = 2 * t + u
                rows = pl.ds(pl.multiple_of(g * GROUP, GROUP), GROUP)
                for k in range(LINES):
                    lines[pl.ds(pl.multiple_of((g * LINES + k) * GROUP, GROUP), GROUP), :] = blocks_ref[
                        rows, 128 * k : 128 * (k + 1)
                    ].astype(F32)

    low = low_half((LINES, 128))

    def block(place):
        slot = slots_ref[place]
        used = jnp.maximum(slot, 0)
        first = lax.div(used, GROUP) * (GROUP * LINES) + lax.rem(used, GROUP)
        value = lines[pl.ds(first, LINES, stride=GROUP), :]
        return jnp.where(slot >= 0, value, jnp.zeros_like(value))

    def pair(place, n):
        a, b = block(place), block(place + 1)
        mixed[pl.ds(n * BLOCK, LINES, stride=2), :] = jnp.where(low, a, pltpu.roll(b, BLOCK, 1))
        mixed[pl.ds(n * BLOCK + 1, LINES, stride=2), :] = jnp.where(low, pltpu.roll(a, BLOCK, 1), b)

    short = min(row_blocks, col_blocks)
    pairs = mixed.shape[0] // BLOCK

    def dense(n):
        return mixed[n * BLOCK : (n + 1) * BLOCK, :].astype(BF16)

    if row_major:
        rows = out_ref.shape[0] // BLOCK
        across = short // 2
        down = pairs // across

        @pl.loop(0, rows // down)
        def _(t):
            for n in range(pairs):
                pair((step * rows + t * down + n // across) * col_blocks + 2 * (n % across), n)
            for n in range(pairs):
                out_ref[
                    pl.ds(pl.multiple_of((t * down + n // across) * BLOCK, BLOCK), BLOCK),
                    (n % across) * 128 : (n % across + 1) * 128,
                ] = dense(n)
    else:
        cols = out_ref.shape[1] // 128
        across = pairs // short

        @pl.loop(0, cols // across)
        def _(t):
            for n in range(pairs):
                pair((n % short) * col_blocks + (step * cols + t * across + n // short) * 2, n)
            for n in range(pairs):
                out_ref[
                    (n % short) * BLOCK : (n % short + 1) * BLOCK,
                    pl.ds(pl.multiple_of((t * across + n // short) * 128, 128), 128),
                ] = dense(n)


def densify(blocks, block_index, live_count, row_blocks, col_blocks):
    slot_count = blocks.shape[0]
    slots = jnp.arange(slot_count, dtype=jnp.int32)
    places = jnp.arange(row_blocks * col_blocks, dtype=jnp.int32)
    hit = (block_index[None, :] == places[:, None]) & (slots < live_count)[None, :]
    slot_of_place = jnp.max(jnp.where(hit, slots[None, :], -1), axis=1)
    row_major = row_blocks > col_blocks
    steps = 8
    rows, cols = row_blocks * BLOCK, col_blocks * BLOCK
    if row_major:
        out_spec = pl.BlockSpec((rows // steps, cols), lambda i, *_: (i, 0))
    else:
        out_spec = pl.BlockSpec((rows, cols // steps), lambda i, *_: (0, i))
    return pl.pallas_call(
        functools.partial(place_kernel, row_major=row_major, row_blocks=row_blocks, col_blocks=col_blocks),
        out_shape=jax.ShapeDtypeStruct((rows, cols), blocks.dtype),
        grid_spec=pltpu.PrefetchScalarGridSpec(
            num_scalar_prefetch=1,
            grid=(steps,),
            in_specs=[pl.BlockSpec(blocks.shape, lambda i, *_: (0, 0), pipeline_mode=pl.Buffered(1))],
            out_specs=out_spec,
            scratch_shapes=[
                pltpu.VMEM((slot_count * LINES, 128), F32),
                pltpu.VMEM((PAIRS * BLOCK, 128), F32),
            ],
        ),
        compiler_params=pltpu.CompilerParams(vmem_limit_bytes=VMEM_LIMIT),
    )(slot_of_place, blocks)


def weight_grad_kernel(index_ref, count_ref, lhs_ref, rhs_ref, out_ref, dense, lines, *, up, col_blocks):
    step = pl.program_id(0)
    product = lax.dot_general(lhs_ref[0], rhs_ref[0], (((0,), (0,)), ((), ())), preferred_element_type=F32)
    height, width = product.shape
    chunks = width // 128
    column = height * pl.num_programs(0) if up else height
    for j in range(chunks):
        first = j * column + step * height if up else (step * chunks + j) * column
        dense[pl.ds(pl.multiple_of(first, 128), height), :] = product[:, 128 * j : 128 * (j + 1)]

    @pl.when(step == pl.num_programs(0) - 1)
    def _():
        count = count_ref[0]
        low = low_half((LINES, 128))

        @pl.loop(0, out_ref.shape[0] // GROUP)
        def _(g):
            for i in range(GROUP):
                slot = g * GROUP + i
                place = index_ref[slot]
                block_row, block_col = lax.div(place, col_blocks), lax.rem(place, col_blocks)
                first = lax.div(block_col, 2) * column + block_row * BLOCK
                odd = lax.rem(block_col, 2)
                even_rows = dense[pl.ds(first, LINES, stride=2), :]
                odd_rows = dense[pl.ds(first + 1, LINES, stride=2), :]
                value = jnp.where(
                    low,
                    jnp.where(odd == 1, pltpu.roll(even_rows, BLOCK, 1), even_rows),
                    jnp.where(odd == 1, odd_rows, pltpu.roll(odd_rows, BLOCK, 1)),
                )
                lines[pl.ds(i, LINES, stride=GROUP), :] = jnp.where(slot < count, value, jnp.zeros_like(value))
            rows = pl.ds(pl.multiple_of(g * GROUP, GROUP), GROUP)
            for k in range(LINES):
                out_ref[rows, 128 * k : 128 * (k + 1)] = lines[k * GROUP : (k + 1) * GROUP, :].astype(BF16)


def weight_grad(lhs, rhs, block_index, live_count, up, col_blocks):
    halves, tokens, width = (lhs if up else rhs).shape
    units = (rhs if up else lhs).shape[2]
    tile = TILE
    per_half = width // tile
    wide = pl.BlockSpec((1, tokens, tile), lambda i, *_: (i // per_half, 0, i % per_half))
    narrow = pl.BlockSpec((1, tokens, units), lambda i, *_: (i // per_half, 0, 0))
    slots = block_index.shape[0]
    return pl.pallas_call(
        functools.partial(weight_grad_kernel, up=up, col_blocks=col_blocks),
        out_shape=jax.ShapeDtypeStruct((slots, BLOCK * BLOCK), BF16),
        grid_spec=pltpu.PrefetchScalarGridSpec(
            num_scalar_prefetch=2,
            grid=(halves * per_half,),
            in_specs=[wide, narrow] if up else [narrow, wide],
            out_specs=pl.BlockSpec((slots, BLOCK * BLOCK), lambda i, *_: (0, 0), pipeline_mode=pl.Buffered(1)),
            scratch_shapes=[
                pltpu.VMEM((units * halves * width // 128, 128), F32),
                pltpu.VMEM((LINES * GROUP, 128), F32),
            ],
        ),
        compiler_params=pltpu.CompilerParams(vmem_limit_bytes=VMEM_LIMIT),
    )(block_index, live_count, lhs, rhs)


CHUNKS = 2


def layers_kernel(
    inp, cot, gain_ref, w_up_hbm, w_down_hbm,
    outs, grads, normed_hbm, grad_hbm, hid_out, ug_out,
    w_up, w_down, xin, gin, ibuf, gath, part, xbuf, sbuf, obuf, rsend, rbuf, ya, yb, up_keep, act_keep, tmp,
    w_sem, keep_sem, sec_send, sec_recv, p1_send, p1_recv, p2_send, p2_recv, sib_send, sib_recv,
    r0_send, r0_recv, r1_send, r1_recv, r2_send, r2_recv,
):
    micro, toks, features = inp.shape
    half = features // 2
    width = half // CHUNKS
    slab = SIDE * toks
    core_rows = SIDE * slab
    tokens = CORES * core_rows
    section, tp = lax.axis_index("section"), lax.axis_index("tp")
    sections = lax.axis_size("section")
    core = lax.rem(tp, CORES)
    y = lax.rem(lax.div(tp, CORES), SIDE)
    z = lax.div(tp, CORES * SIDE)
    sibling = {"tp": tp + 1 - 2 * core}
    inner = (z, y)
    outer = (y, z)
    SENDING, WAITING = (2, 1, 3), (1, 3, 2)

    def at(zz, yy):
        return {"tp": (zz * SIDE + yy) * CORES + core}

    def inner_peer(h, k):
        i = lax.rem(inner[h] + k, SIDE)
        return i, (at(i, y) if h == 0 else at(z, i))

    def outer_peer(h, k):
        o = lax.rem(outer[h] + k, SIDE)
        return o, (at(z, o) if h == 0 else at(o, y))

    def remote(src, dst, send, recv, device):
        return pltpu.make_async_remote_copy(
            src_ref=src, dst_ref=dst, send_sem=send, recv_sem=recv, device_id=device, device_id_type=MESH
        )

    load_up = pltpu.make_async_copy(w_up_hbm, w_up, w_sem.at[0])
    load_down = pltpu.make_async_copy(w_down_hbm, w_down, w_sem.at[1])
    load_up.start()
    load_down.start()

    barrier = pltpu.get_barrier_semaphore()
    peers = [sibling]
    for h in range(2):
        peers += [inner_peer(h, k)[1] for k in range(1, SIDE)]
    for peer in peers:
        pl.semaphore_signal(barrier, inc=1, device_id=peer, device_id_type=MESH)

    @pl.when(section > 0)
    def _():
        pl.semaphore_signal(barrier, inc=1, device_id={"section": section - 1}, device_id_type=MESH)

    @pl.when(section < sections - 1)
    def _():
        pl.semaphore_signal(barrier, inc=1, device_id={"section": section + 1}, device_id_type=MESH)

    @pl.when((section == 0) | (section == sections - 1))
    def _():
        pl.semaphore_wait(barrier, len(peers) + 1)

    @pl.when((section > 0) & (section < sections - 1))
    def _():
        pl.semaphore_wait(barrier, len(peers) + 2)

    def core_slabs(c):
        return pl.ds(pl.multiple_of(c * core_rows, core_rows), core_rows)

    def slab_rows(o, c):
        return pl.ds(pl.multiple_of((c * SIDE + o) * slab, slab), slab)

    def first_copies(job, h):
        ref = ibuf.at[job, h, pl.ds(0, SIDE - 1)]
        return remote(ref, ref, p1_send.at[job, h], p1_recv.at[job, h], sibling)

    def second_sends(job, h):
        ref = gath.at[job, h, pl.ds(0, (SIDE - 1) * slab)]
        return remote(ref, ref, p2_send.at[job, h], p2_recv.at[job, h, 0], sibling)

    def sibling_copies(job, h):
        ref = gath.at[job, h, core_slabs(1 - core)]
        return remote(ref, ref, sib_send.at[job, h], sib_recv.at[job, h], sibling)

    def exchange(job, h, q):
        return remote(
            part.at[h, q, core_slabs(1 - core)],
            xbuf.at[job, h, q],
            r0_send.at[job, h, q],
            r0_recv.at[job, h, q],
            sibling,
        )

    def outer_copies(job, h, q):
        ref = obuf.at[job, h, q]
        return remote(ref, ref, r1_send.at[job, h, q], r1_recv.at[job, h, q], sibling)

    def inner_copies(job, h):
        ref = rbuf.at[job, h]
        return remote(ref, ref, r2_send.at[job, h], r2_recv.at[job, h], sibling)

    def gather(job, values):
        for h in range(2):
            mine = ibuf.at[job, h, inner[h]]
            mine[...] = values[:, h * half : (h + 1) * half].astype(BF16)
            for k in SENDING:
                remote(mine, mine, p1_send.at[job, h], p1_recv.at[job, h], inner_peer(h, k)[1]).start()
        second = {}
        for h in range(2):
            first_copies(job, h).wait_recv()
            for i in range(SIDE):
                tmp[h, i * toks : (i + 1) * toks, :] = ibuf[job, h, i].astype(F32)
            rows = slab_rows(outer[h], core)
            gath[job, h, rows, :] = tmp[h].astype(BF16)
            mine = gath.at[job, h, rows]
            for k in SENDING:
                copy = remote(mine, mine, p2_send.at[job, h], p2_recv.at[job, h, k - 1], outer_peer(h, k)[1])
                copy.start()
                second[h, k] = copy
            remote(mine, mine, sib_send.at[job, h], sib_recv.at[job, h], sibling).start()
        for k in WAITING:
            for h in range(2):
                second[h, k].wait_recv()
                came = gath.at[job, h, slab_rows(outer_peer(h, SIDE - k)[0], core)]
                remote(came, came, sib_send.at[job, h], sib_recv.at[job, h], sibling).start()

    def keep(job, mb, rows_hbm):
        return [
            pltpu.make_async_copy(
                gath.at[job, h],
                rows_hbm.at[h, pl.ds(pl.multiple_of(mb * tokens, tokens), tokens)],
                keep_sem.at[job, h],
            )
            for h in range(2)
        ]

    def permuted(target, source, add):
        for c in range(CORES):
            for a in range(SIDE):
                for b in range(SIDE):
                    to, of = ((c * SIDE + a) * SIDE + b) * toks, ((c * SIDE + b) * SIDE + a) * toks
                    moved = source[of : of + toks, :]
                    target[to : to + toks, :] = target[to : to + toks, :] + moved if add else moved

    def scatter(job, product):
        def spread(h, q):
            exchange(job, h, q).wait_recv()
            sbuf[job, h, q] = part[h, q, core_slabs(core), :] + xbuf[job, h, q]
            for k in SENDING:
                o, peer = outer_peer(h, k)
                remote(
                    sbuf.at[job, h, q, pl.ds(pl.multiple_of(o * slab, slab), slab)],
                    obuf.at[job, h, q, k - 1],
                    r1_send.at[job, h, q],
                    r1_recv.at[job, h, q],
                    peer,
                ).start()

        steps = [(h, q) for q in range(CHUNKS) for h in range(2)]
        for n, (h, q) in enumerate(steps):
            part[h, q] = product(h, q).astype(BF16)
            exchange(job, h, q).start()
            if n:
                spread(*steps[n - 1])
        spread(*steps[-1])
        for h in range(2):
            for q in range(CHUNKS):
                outer_copies(job, h, q).wait_recv()
                own = sbuf[job, h, q, pl.ds(pl.multiple_of(outer[h] * slab, slab), slab), :].astype(F32)
                came = [obuf[job, h, q, k].astype(F32) for k in range(SIDE - 1)]
                tmp[h, :, q * width : (q + 1) * width] = own + (came[0] + came[1] + came[2])
            for i in range(SIDE):
                rsend[job, h, i] = tmp[h, i * toks : (i + 1) * toks, :].astype(BF16)
            for k in SENDING:
                i, peer = inner_peer(h, k)
                remote(
                    rsend.at[job, h, i], rbuf.at[job, h, k - 1], r2_send.at[job, h], r2_recv.at[job, h], peer
                ).start()
        for h, q in steps:
            exchange(job, h, q).wait_send()
        sums = []
        for h in range(2):
            inner_copies(job, h).wait_recv()
            came = [rbuf[job, h, k].astype(F32) for k in range(SIDE - 1)]
            sums.append(rsend[job, h, inner[h]].astype(F32) + (came[0] + came[1] + came[2]))
        return jnp.concatenate(sums, axis=1)

    gain = gain_ref[...].astype(F32)
    NT = (((1,), (1,)), ((), ()))

    def columns(h, q=0, size=half):
        return slice(h * half + q * size, h * half + (q + 1) * size)

    def forward_in(mb):
        return remote(outs.at[mb], xin.at[mb], sec_send.at[0, mb], sec_recv.at[0, mb], {"section": section + 1})

    def backward_in(mb):
        return remote(grads.at[mb], gin.at[mb], sec_send.at[1, mb], sec_recv.at[1, mb], {"section": section - 1})

    def norm(mb):
        values = xin[mb].astype(F32)
        inv_rms = lax.rsqrt(jnp.mean(values * values, axis=-1, keepdims=True) + NORM_EPSILON)
        return values, inv_rms

    def forward(mb, _):
        job = mb

        @pl.when(section == 0)
        def _():
            xin[mb] = inp[mb]

        @pl.when(section > 0)
        def _():
            forward_in(mb).wait_recv()

        values, inv_rms = norm(mb)
        gather(job, values * inv_rms * gain)

        @pl.when((mb == 0) & (section < sections - 1))
        def _():
            load_up.wait()
            load_down.wait()

        for h, acc in ((0, ya), (1, yb)):
            sibling_copies(job, h).wait_recv()
            acc[...] = jnp.dot(gath[job, h], w_up[columns(h), :], preferred_element_type=F32)

        permuted(ya, yb, True)
        up = ya[...]
        up_keep[mb] = up
        hidden = up / (1.0 + jnp.exp(-up))
        ya[...] = hidden
        permuted(yb, ya, False)
        kept = pl.ds(pl.multiple_of(mb * tokens, tokens), tokens)
        for h, acc in ((0, ya), (1, yb)):
            hid_out[h, kept, :] = acc[...].astype(BF16)

        def product(h, q):
            return jnp.dot(hid_out[h, kept, :], w_down[:, columns(h, q, width)], preferred_element_type=F32)

        mixed = scatter(job, product)
        outs[mb] = (xin[mb].astype(F32) + mixed).astype(BF16)

        @pl.when(section < sections - 1)
        def _():
            forward_in(mb).start()

        for copy in keep(job, mb, normed_hbm):
            copy.start()
        return 0

    def hidden_grad(mb):
        job = micro + mb
        gather(job, gin[mb].astype(F32))
        for h, acc in ((0, ya), (1, yb)):
            sibling_copies(job, h).wait_recv()
            acc[...] = lax.dot_general(gath[job, h], w_down[:, columns(h)], NT, preferred_element_type=F32)
        for copy in keep(job, mb, grad_hbm):
            copy.start()
        permuted(ya, yb, True)
        act_keep[mb] = ya[...]

    def backward(mb, _):
        job = micro + mb

        @pl.when(section < sections - 1)
        def _():
            backward_in(mb).wait_recv()
            hidden_grad(mb)

        up = up_keep[mb]
        q = 1.0 / (1.0 + jnp.exp(-up))
        ya[...] = act_keep[mb] * q * (1.0 + up * (1.0 - q))
        permuted(yb, ya, False)
        kept = pl.ds(pl.multiple_of(mb * tokens, tokens), tokens)
        for h, acc in ((0, ya), (1, yb)):
            ug_out[h, kept, :] = acc[...].astype(BF16)

        def product(h, q):
            return lax.dot_general(ug_out[h, kept, :], w_up[columns(h, q, width), :], NT, preferred_element_type=F32)

        scaled = scatter(job, product) * gain
        values, inv_rms = norm(mb)
        term = inv_rms * scaled - values * (inv_rms * inv_rms * inv_rms) * jnp.mean(
            scaled * values, axis=-1, keepdims=True
        )
        grads[mb] = (gin[mb].astype(F32) + term).astype(BF16)

        @pl.when(section > 0)
        def _():
            backward_in(mb).start()

        return 0

    @pl.when(section == sections - 1)
    def _():
        load_up.wait()
        load_down.wait()
        gin[...] = cot[...]

        @pl.loop(0, micro)
        def _(mb):
            hidden_grad(mb)

    lax.fori_loop(0, micro, forward, 0)
    lax.fori_loop(0, micro, backward, 0)

    for mb in range(micro):
        for copy in keep(mb, mb, normed_hbm) + keep(micro + mb, mb, grad_hbm):
            copy.wait()
    for job in range(2 * micro):
        for h in range(2):
            for copies in (first_copies, second_sends, sibling_copies, inner_copies):
                copies(job, h).wait_send()
            for q in range(CHUNKS):
                outer_copies(job, h, q).wait_send()

    @pl.when(section < sections - 1)
    def _():
        for mb in range(micro):
            forward_in(mb).wait_send()

    @pl.when(section > 0)
    def _():
        for mb in range(micro):
            backward_in(mb).wait_send()


def layers(inputs, cotangent, gain, w_up, w_down):
    micro, toks, features = inputs.shape
    half, units, slab, jobs = features // 2, w_up.shape[1], SIDE * toks, 2 * micro
    core_rows, width = slab * SIDE, half // CHUNKS
    tokens = core_rows * CORES
    vmem = pl.BlockSpec(memory_space=pltpu.VMEM)
    hbm = pl.BlockSpec(memory_space=pl.ANY)
    dma = pltpu.SemaphoreType.DMA
    small = jax.ShapeDtypeStruct(inputs.shape, BF16)
    wide = jax.ShapeDtypeStruct((2, micro * tokens, half), BF16)
    narrow = jax.ShapeDtypeStruct((2, micro * tokens, units), BF16)
    return pl.pallas_call(
        layers_kernel,
        out_shape=(small, small, wide, wide, narrow, narrow),
        in_specs=[vmem, vmem, vmem, hbm, hbm],
        out_specs=(vmem, vmem, hbm, hbm, vmem, vmem),
        scratch_shapes=[
            pltpu.VMEM(w_up.shape, BF16),
            pltpu.VMEM(w_down.shape, BF16),
            pltpu.VMEM(inputs.shape, BF16),
            pltpu.VMEM(inputs.shape, BF16),
            pltpu.VMEM((jobs, 2, SIDE, toks, half), BF16),
            pltpu.VMEM((jobs, 2, tokens, half), BF16),
            pltpu.VMEM((2, CHUNKS, tokens, width), BF16),
            pltpu.VMEM((jobs, 2, CHUNKS, core_rows, width), BF16),
            pltpu.VMEM((jobs, 2, CHUNKS, core_rows, width), BF16),
            pltpu.VMEM((jobs, 2, CHUNKS, SIDE - 1, slab, width), BF16),
            pltpu.VMEM((jobs, 2, SIDE, toks, half), BF16),
            pltpu.VMEM((jobs, 2, SIDE - 1, toks, half), BF16),
            pltpu.VMEM((tokens, units), F32),
            pltpu.VMEM((tokens, units), F32),
            pltpu.VMEM((micro, tokens, units), F32),
            pltpu.VMEM((micro, tokens, units), F32),
            pltpu.VMEM((2, slab, half), F32),
            dma((2,)),
            dma((jobs, 2)),
            dma((2, micro)),
            dma((2, micro)),
            dma((jobs, 2)),
            dma((jobs, 2)),
            dma((jobs, 2)),
            dma((jobs, 2, SIDE - 1)),
            dma((jobs, 2)),
            dma((jobs, 2)),
            dma((jobs, 2, CHUNKS)),
            dma((jobs, 2, CHUNKS)),
            dma((jobs, 2, CHUNKS)),
            dma((jobs, 2, CHUNKS)),
            dma((jobs, 2)),
            dma((jobs, 2)),
        ],
        compiler_params=pltpu.CompilerParams(
            collective_id=0, has_side_effects=True, vmem_limit_bytes=VMEM_LIMIT
        ),
    )(inputs, cotangent, gain, w_up, w_down)


def shards(
    inputs, cotangent, gains, up_blocks, up_index, up_count, down_blocks, down_index, down_count
):
    features = inputs.shape[2]
    row_blocks = features // BLOCK
    group_blocks = FF // lax.axis_size("tp") // BLOCK
    w_up = densify(up_blocks[0], up_index[0], up_count[0, 0], row_blocks, group_blocks)
    w_down = densify(down_blocks[0], down_index[0], down_count[0, 0], group_blocks, row_blocks)
    outs, grads, normed, grad_rows, hidden, up_grad = layers(inputs, cotangent, gains, w_up, w_down)
    up_grads = weight_grad(normed, up_grad, up_index[0], up_count[0], True, group_blocks)
    down_grads = weight_grad(hidden, grad_rows, down_index[0], down_count[0], False, row_blocks)
    return (
        outs[None],
        grads[None],
        up_grads[None],
        down_grads[None],
    )


def solution(mesh):
    return jax.shard_map(
        shards,
        mesh=mesh,
        in_specs=(
            P(None, "tp", None),
            P(None, "tp", None),
            P("section", None),
            P("section", "tp", None),
            P("section", "tp"),
            P("section", "tp"),
            P("section", "tp", None),
            P("section", "tp"),
            P("section", "tp"),
        ),
        out_specs=(
            P("section", None, "tp", None),
            P("section", None, "tp", None),
            P("section", "tp", None),
            P("section", "tp", None),
        ),
        check_vma=False,
    )
```

```python
import functools

import jax
import jax.numpy as jnp
from jax import lax
from jax.experimental import pallas as pl
from jax.experimental.pallas import tpu as pltpu
from jax.sharding import PartitionSpec as P

FF = 16384
BLOCK = 64
NORM_EPSILON = 1e-05
MESH = pl.DeviceIdType.MESH
F32 = jnp.float32
BF16 = jnp.bfloat16
SIDE = 4
CORES = 2


LINES = BLOCK * BLOCK // 128
GROUP = 16
VMEM_LIMIT = 60 << 20
TILE = 2048
PAIRS = 32


def low_half(shape):
    return lax.broadcasted_iota(jnp.int32, shape, 1) < BLOCK


def place_kernel(slots_ref, blocks_ref, out_ref, lines, mixed, *, row_major, row_blocks, col_blocks):
    step = pl.program_id(0)

    @pl.when(step == 0)
    def _():
        @pl.loop(0, blocks_ref.shape[0] // (2 * GROUP))
        def _(t):
            for u in range(2):
                g = 2 * t + u
                rows = pl.ds(pl.multiple_of(g * GROUP, GROUP), GROUP)
                for k in range(LINES):
                    lines[pl.ds(pl.multiple_of((g * LINES + k) * GROUP, GROUP), GROUP), :] = blocks_ref[
                        rows, 128 * k : 128 * (k + 1)
                    ].astype(F32)

    low = low_half((LINES, 128))

    def block(place):
        slot = slots_ref[place]
        used = jnp.maximum(slot, 0)
        first = lax.div(used, GROUP) * (GROUP * LINES) + lax.rem(used, GROUP)
        value = lines[pl.ds(first, LINES, stride=GROUP), :]
        return jnp.where(slot >= 0, value, jnp.zeros_like(value))

    def pair(place, n):
        a, b = block(place), block(place + 1)
        mixed[pl.ds(n * BLOCK, LINES, stride=2), :] = jnp.where(low, a, pltpu.roll(b, BLOCK, 1))
        mixed[pl.ds(n * BLOCK + 1, LINES, stride=2), :] = jnp.where(low, pltpu.roll(a, BLOCK, 1), b)

    short = min(row_blocks, col_blocks)
    pairs = mixed.shape[0] // BLOCK

    def dense(n):
        return mixed[n * BLOCK : (n + 1) * BLOCK, :].astype(BF16)

    if row_major:
        rows = out_ref.shape[0] // BLOCK
        across = short // 2
        down = pairs // across

        @pl.loop(0, rows // down)
        def _(t):
            for n in range(pairs):
                pair((step * rows + t * down + n // across) * col_blocks + 2 * (n % across), n)
            for n in range(pairs):
                out_ref[
                    pl.ds(pl.multiple_of((t * down + n // across) * BLOCK, BLOCK), BLOCK),
                    (n % across) * 128 : (n % across + 1) * 128,
                ] = dense(n)
    else:
        cols = out_ref.shape[1] // 128
        across = pairs // short

        @pl.loop(0, cols // across)
        def _(t):
            for n in range(pairs):
                pair((n % short) * col_blocks + (step * cols + t * across + n // short) * 2, n)
            for n in range(pairs):
                out_ref[
                    (n % short) * BLOCK : (n % short + 1) * BLOCK,
                    pl.ds(pl.multiple_of((t * across + n // short) * 128, 128), 128),
                ] = dense(n)


def densify(blocks, block_index, live_count, row_blocks, col_blocks):
    slot_count = blocks.shape[0]
    slots = jnp.arange(slot_count, dtype=jnp.int32)
    places = jnp.arange(row_blocks * col_blocks, dtype=jnp.int32)
    hit = (block_index[None, :] == places[:, None]) & (slots < live_count)[None, :]
    slot_of_place = jnp.max(jnp.where(hit, slots[None, :], -1), axis=1)
    row_major = row_blocks > col_blocks
    steps = 8
    rows, cols = row_blocks * BLOCK, col_blocks * BLOCK
    if row_major:
        out_spec = pl.BlockSpec((rows // steps, cols), lambda i, *_: (i, 0))
    else:
        out_spec = pl.BlockSpec((rows, cols // steps), lambda i, *_: (0, i))
    return pl.pallas_call(
        functools.partial(place_kernel, row_major=row_major, row_blocks=row_blocks, col_blocks=col_blocks),
        out_shape=jax.ShapeDtypeStruct((rows, cols), blocks.dtype),
        grid_spec=pltpu.PrefetchScalarGridSpec(
            num_scalar_prefetch=1,
            grid=(steps,),
            in_specs=[pl.BlockSpec(blocks.shape, lambda i, *_: (0, 0), pipeline_mode=pl.Buffered(1))],
            out_specs=out_spec,
            scratch_shapes=[
                pltpu.VMEM((slot_count * LINES, 128), F32),
                pltpu.VMEM((PAIRS * BLOCK, 128), F32),
            ],
        ),
        compiler_params=pltpu.CompilerParams(vmem_limit_bytes=VMEM_LIMIT),
    )(slot_of_place, blocks)


def weight_grad_kernel(index_ref, count_ref, lhs_ref, rhs_ref, out_ref, dense, lines, *, up, col_blocks):
    step = pl.program_id(0)
    product = lax.dot_general(lhs_ref[0], rhs_ref[0], (((0,), (0,)), ((), ())), preferred_element_type=F32)
    height, width = product.shape
    chunks = width // 128
    column = height * pl.num_programs(0) if up else height
    for j in range(chunks):
        first = j * column + step * height if up else (step * chunks + j) * column
        dense[pl.ds(pl.multiple_of(first, 128), height), :] = product[:, 128 * j : 128 * (j + 1)]

    @pl.when(step == pl.num_programs(0) - 1)
    def _():
        count = count_ref[0]
        low = low_half((LINES, 128))

        @pl.loop(0, out_ref.shape[0] // GROUP)
        def _(g):
            for i in range(GROUP):
                slot = g * GROUP + i
                place = index_ref[slot]
                block_row, block_col = lax.div(place, col_blocks), lax.rem(place, col_blocks)
                first = lax.div(block_col, 2) * column + block_row * BLOCK
                odd = lax.rem(block_col, 2)
                even_rows = dense[pl.ds(first, LINES, stride=2), :]
                odd_rows = dense[pl.ds(first + 1, LINES, stride=2), :]
                value = jnp.where(
                    low,
                    jnp.where(odd == 1, pltpu.roll(even_rows, BLOCK, 1), even_rows),
                    jnp.where(odd == 1, odd_rows, pltpu.roll(odd_rows, BLOCK, 1)),
                )
                lines[pl.ds(i, LINES, stride=GROUP), :] = jnp.where(slot < count, value, jnp.zeros_like(value))
            rows = pl.ds(pl.multiple_of(g * GROUP, GROUP), GROUP)
            for k in range(LINES):
                out_ref[rows, 128 * k : 128 * (k + 1)] = lines[k * GROUP : (k + 1) * GROUP, :].astype(BF16)


def weight_grad(lhs, rhs, block_index, live_count, up, col_blocks):
    halves, tokens, width = (lhs if up else rhs).shape
    units = (rhs if up else lhs).shape[2]
    tile = TILE
    per_half = width // tile
    wide = pl.BlockSpec((1, tokens, tile), lambda i, *_: (i // per_half, 0, i % per_half))
    narrow = pl.BlockSpec((1, tokens, units), lambda i, *_: (i // per_half, 0, 0))
    slots = block_index.shape[0]
    return pl.pallas_call(
        functools.partial(weight_grad_kernel, up=up, col_blocks=col_blocks),
        out_shape=jax.ShapeDtypeStruct((slots, BLOCK * BLOCK), BF16),
        grid_spec=pltpu.PrefetchScalarGridSpec(
            num_scalar_prefetch=2,
            grid=(halves * per_half,),
            in_specs=[wide, narrow] if up else [narrow, wide],
            out_specs=pl.BlockSpec((slots, BLOCK * BLOCK), lambda i, *_: (0, 0), pipeline_mode=pl.Buffered(1)),
            scratch_shapes=[
                pltpu.VMEM((units * halves * width // 128, 128), F32),
                pltpu.VMEM((LINES * GROUP, 128), F32),
            ],
        ),
        compiler_params=pltpu.CompilerParams(vmem_limit_bytes=VMEM_LIMIT),
    )(block_index, live_count, lhs, rhs)


CHUNKS = 2


def layers_kernel(
    inp, cot, gain_ref, w_up_hbm, w_down_hbm,
    outs, grads, normed_hbm, grad_hbm, hid_out, ug_out,
    w_up, w_down, xin, gin, ibuf, gath, part, xbuf, sbuf, obuf, rsend, rbuf, ya, yb, up_keep, act_keep, tmp,
    w_sem, keep_sem, sec_send, sec_recv, p1_send, p1_recv, p2_send, p2_recv, sib_send, sib_recv,
    r0_send, r0_recv, r1_send, r1_recv, r2_send, r2_recv,
):
    micro, toks, features = inp.shape
    half = features // 2
    width = half // CHUNKS
    slab = SIDE * toks
    core_rows = SIDE * slab
    tokens = CORES * core_rows
    section, tp = lax.axis_index("section"), lax.axis_index("tp")
    sections = lax.axis_size("section")
    core = lax.rem(tp, CORES)
    y = lax.rem(lax.div(tp, CORES), SIDE)
    z = lax.div(tp, CORES * SIDE)
    sibling = {"tp": tp + 1 - 2 * core}
    inner = (z, y)
    outer = (y, z)
    SENDING, WAITING = (2, 1, 3), (1, 3, 2)

    def at(zz, yy):
        return {"tp": (zz * SIDE + yy) * CORES + core}

    def inner_peer(h, k):
        i = lax.rem(inner[h] + k, SIDE)
        return i, (at(i, y) if h == 0 else at(z, i))

    def outer_peer(h, k):
        o = lax.rem(outer[h] + k, SIDE)
        return o, (at(z, o) if h == 0 else at(o, y))

    def remote(src, dst, send, recv, device):
        return pltpu.make_async_remote_copy(
            src_ref=src, dst_ref=dst, send_sem=send, recv_sem=recv, device_id=device, device_id_type=MESH
        )

    load_up = pltpu.make_async_copy(w_up_hbm, w_up, w_sem.at[0])
    load_down = pltpu.make_async_copy(w_down_hbm, w_down, w_sem.at[1])
    load_up.start()
    load_down.start()

    barrier = pltpu.get_barrier_semaphore()
    peers = [sibling]
    for h in range(2):
        peers += [inner_peer(h, k)[1] for k in range(1, SIDE)]
    for peer in peers:
        pl.semaphore_signal(barrier, inc=1, device_id=peer, device_id_type=MESH)

    @pl.when(section > 0)
    def _():
        pl.semaphore_signal(barrier, inc=1, device_id={"section": section - 1}, device_id_type=MESH)

    @pl.when(section < sections - 1)
    def _():
        pl.semaphore_signal(barrier, inc=1, device_id={"section": section + 1}, device_id_type=MESH)

    @pl.when((section == 0) | (section == sections - 1))
    def _():
        pl.semaphore_wait(barrier, len(peers) + 1)

    @pl.when((section > 0) & (section < sections - 1))
    def _():
        pl.semaphore_wait(barrier, len(peers) + 2)

    def core_slabs(c):
        return pl.ds(pl.multiple_of(c * core_rows, core_rows), core_rows)

    def slab_rows(o, c):
        return pl.ds(pl.multiple_of((c * SIDE + o) * slab, slab), slab)

    def first_copies(job, h):
        ref = ibuf.at[job, h, pl.ds(0, SIDE - 1)]
        return remote(ref, ref, p1_send.at[job, h], p1_recv.at[job, h], sibling)

    def second_sends(job, h):
        ref = gath.at[job, h, pl.ds(0, (SIDE - 1) * slab)]
        return remote(ref, ref, p2_send.at[job, h], p2_recv.at[job, h, 0], sibling)

    def sibling_copies(job, h):
        ref = gath.at[job, h, core_slabs(1 - core)]
        return remote(ref, ref, sib_send.at[job, h], sib_recv.at[job, h], sibling)

    def exchange(job, h, q):
        return remote(
            part.at[h, q, core_slabs(1 - core)],
            xbuf.at[job, h, q],
            r0_send.at[job, h, q],
            r0_recv.at[job, h, q],
            sibling,
        )

    def outer_copies(job, h, q):
        ref = obuf.at[job, h, q]
        return remote(ref, ref, r1_send.at[job, h, q], r1_recv.at[job, h, q], sibling)

    def inner_copies(job, h):
        ref = rbuf.at[job, h]
        return remote(ref, ref, r2_send.at[job, h], r2_recv.at[job, h], sibling)

    def second_copy(job, h, k):
        mine = gath.at[job, h, slab_rows(outer[h], core)]
        return remote(mine, mine, p2_send.at[job, h], p2_recv.at[job, h, k - 1], outer_peer(h, k)[1])

    def gather_first(job, values):
        for h in range(2):
            mine = ibuf.at[job, h, inner[h]]
            mine[...] = values[:, h * half : (h + 1) * half].astype(BF16)
            for k in SENDING:
                remote(mine, mine, p1_send.at[job, h], p1_recv.at[job, h], inner_peer(h, k)[1]).start()

    def gather_second(job):
        for h in range(2):
            first_copies(job, h).wait_recv()
            for i in range(SIDE):
                tmp[h, i * toks : (i + 1) * toks, :] = ibuf[job, h, i].astype(F32)
            rows = slab_rows(outer[h], core)
            gath[job, h, rows, :] = tmp[h].astype(BF16)
            mine = gath.at[job, h, rows]
            for k in SENDING:
                second_copy(job, h, k).start()
            remote(mine, mine, sib_send.at[job, h], sib_recv.at[job, h], sibling).start()

    def gather_third(job):
        for k in WAITING:
            for h in range(2):
                second_copy(job, h, k).wait_recv()
                came = gath.at[job, h, slab_rows(outer_peer(h, SIDE - k)[0], core)]
                remote(came, came, sib_send.at[job, h], sib_recv.at[job, h], sibling).start()

    def keep(job, mb, rows_hbm):
        return [
            pltpu.make_async_copy(
                gath.at[job, h],
                rows_hbm.at[h, pl.ds(pl.multiple_of(mb * tokens, tokens), tokens)],
                keep_sem.at[job, h],
            )
            for h in range(2)
        ]

    def permuted(target, source, add):
        for c in range(CORES):
            for a in range(SIDE):
                for b in range(SIDE):
                    to, of = ((c * SIDE + a) * SIDE + b) * toks, ((c * SIDE + b) * SIDE + a) * toks
                    moved = source[of : of + toks, :]
                    target[to : to + toks, :] = target[to : to + toks, :] + moved if add else moved

    def scatter(job, product, meanwhile, after):
        def spread(h, q):
            exchange(job, h, q).wait_recv()
            sbuf[job, h, q] = part[h, q, core_slabs(core), :] + xbuf[job, h, q]
            for k in SENDING:
                o, peer = outer_peer(h, k)
                remote(
                    sbuf.at[job, h, q, pl.ds(pl.multiple_of(o * slab, slab), slab)],
                    obuf.at[job, h, q, k - 1],
                    r1_send.at[job, h, q],
                    r1_recv.at[job, h, q],
                    peer,
                ).start()

        steps = [(h, q) for q in range(CHUNKS) for h in range(2)]
        for n, (h, q) in enumerate(steps):
            part[h, q] = product(h, q).astype(BF16)
            exchange(job, h, q).start()
            if n:
                spread(*steps[n - 1])
        spread(*steps[-1])
        meanwhile()
        for h in range(2):
            for q in range(CHUNKS):
                outer_copies(job, h, q).wait_recv()
                own = sbuf[job, h, q, pl.ds(pl.multiple_of(outer[h] * slab, slab), slab), :].astype(F32)
                came = [obuf[job, h, q, k].astype(F32) for k in range(SIDE - 1)]
                tmp[h, :, q * width : (q + 1) * width] = own + (came[0] + came[1] + came[2])
            for i in range(SIDE):
                rsend[job, h, i] = tmp[h, i * toks : (i + 1) * toks, :].astype(BF16)
            for k in SENDING:
                i, peer = inner_peer(h, k)
                remote(
                    rsend.at[job, h, i], rbuf.at[job, h, k - 1], r2_send.at[job, h], r2_recv.at[job, h], peer
                ).start()
        after()
        for h, q in steps:
            exchange(job, h, q).wait_send()
        sums = []
        for h in range(2):
            inner_copies(job, h).wait_recv()
            came = [rbuf[job, h, k].astype(F32) for k in range(SIDE - 1)]
            sums.append(rsend[job, h, inner[h]].astype(F32) + (came[0] + came[1] + came[2]))
        return jnp.concatenate(sums, axis=1)

    gain = gain_ref[...].astype(F32)
    NT = (((1,), (1,)), ((), ()))

    def columns(h, q=0, size=half):
        return slice(h * half + q * size, h * half + (q + 1) * size)

    def forward_in(mb):
        return remote(outs.at[mb], xin.at[mb], sec_send.at[0, mb], sec_recv.at[0, mb], {"section": section + 1})

    def backward_in(mb):
        return remote(grads.at[mb], gin.at[mb], sec_send.at[1, mb], sec_recv.at[1, mb], {"section": section - 1})

    def norm(mb):
        values = xin[mb].astype(F32)
        inv_rms = lax.rsqrt(jnp.mean(values * values, axis=-1, keepdims=True) + NORM_EPSILON)
        return values, inv_rms

    def begin_forward(mb):
        @pl.when(section == 0)
        def _():
            xin[mb] = inp[mb]

        @pl.when(section > 0)
        def _():
            forward_in(mb).wait_recv()

        values, inv_rms = norm(mb)
        gather_first(mb, values * inv_rms * gain)

    def forward(mb, _):
        job = mb
        gather_third(job)

        @pl.when((mb == 0) & (section < sections - 1))
        def _():
            load_up.wait()
            load_down.wait()

        for h, acc in ((0, ya), (1, yb)):
            sibling_copies(job, h).wait_recv()
            acc[...] = jnp.dot(gath[job, h], w_up[columns(h), :], preferred_element_type=F32)

        permuted(ya, yb, True)
        up = ya[...]
        up_keep[mb] = up
        hidden = up / (1.0 + jnp.exp(-up))
        ya[...] = hidden
        permuted(yb, ya, False)
        kept = pl.ds(pl.multiple_of(mb * tokens, tokens), tokens)
        for h, acc in ((0, ya), (1, yb)):
            hid_out[h, kept, :] = acc[...].astype(BF16)

        def product(h, q):
            return jnp.dot(hid_out[h, kept, :], w_down[:, columns(h, q, width)], preferred_element_type=F32)

        def meanwhile():
            @pl.when(mb < micro - 1)
            def _():
                begin_forward(mb + 1)

        def after():
            @pl.when(mb < micro - 1)
            def _():
                gather_second(job + 1)

        mixed = scatter(job, product, meanwhile, after)
        outs[mb] = (xin[mb].astype(F32) + mixed).astype(BF16)

        @pl.when(section < sections - 1)
        def _():
            forward_in(mb).start()

        for copy in keep(job, mb, normed_hbm):
            copy.start()
        return 0

    def hidden_grad(mb):
        job = micro + mb
        gather_third(job)
        for h, acc in ((0, ya), (1, yb)):
            sibling_copies(job, h).wait_recv()
            acc[...] = lax.dot_general(gath[job, h], w_down[:, columns(h)], NT, preferred_element_type=F32)
        for copy in keep(job, mb, grad_hbm):
            copy.start()
        permuted(ya, yb, True)
        act_keep[mb] = ya[...]

    def begin_backward(mb):
        backward_in(mb).wait_recv()
        gather_first(micro + mb, gin[mb].astype(F32))

    def backward(mb, _):
        job = micro + mb

        @pl.when(section < sections - 1)
        def _():
            hidden_grad(mb)

        up = up_keep[mb]
        q = 1.0 / (1.0 + jnp.exp(-up))
        ya[...] = act_keep[mb] * q * (1.0 + up * (1.0 - q))
        permuted(yb, ya, False)
        kept = pl.ds(pl.multiple_of(mb * tokens, tokens), tokens)
        for h, acc in ((0, ya), (1, yb)):
            ug_out[h, kept, :] = acc[...].astype(BF16)

        def product(h, q):
            return lax.dot_general(ug_out[h, kept, :], w_up[columns(h, q, width), :], NT, preferred_element_type=F32)

        more = (mb < micro - 1) & (section < sections - 1)

        def meanwhile():
            @pl.when(more)
            def _():
                begin_backward(mb + 1)

        def after():
            @pl.when(more)
            def _():
                gather_second(job + 1)

        scaled = scatter(job, product, meanwhile, after) * gain
        values, inv_rms = norm(mb)
        term = inv_rms * scaled - values * (inv_rms * inv_rms * inv_rms) * jnp.mean(
            scaled * values, axis=-1, keepdims=True
        )
        grads[mb] = (gin[mb].astype(F32) + term).astype(BF16)

        @pl.when(section > 0)
        def _():
            backward_in(mb).start()

        return 0

    @pl.when(section == sections - 1)
    def _():
        load_up.wait()
        load_down.wait()
        gin[...] = cot[...]

        @pl.loop(0, micro)
        def _(mb):
            gather_first(micro + mb, gin[mb].astype(F32))
            gather_second(micro + mb)
            hidden_grad(mb)

    begin_forward(0)
    gather_second(0)
    lax.fori_loop(0, micro, forward, 0)

    @pl.when(section < sections - 1)
    def _():
        begin_backward(0)
        gather_second(micro)

    lax.fori_loop(0, micro, backward, 0)

    for mb in range(micro):
        for copy in keep(mb, mb, normed_hbm) + keep(micro + mb, mb, grad_hbm):
            copy.wait()
    for job in range(2 * micro):
        for h in range(2):
            for copies in (first_copies, second_sends, sibling_copies, inner_copies):
                copies(job, h).wait_send()
            for q in range(CHUNKS):
                outer_copies(job, h, q).wait_send()

    @pl.when(section < sections - 1)
    def _():
        for mb in range(micro):
            forward_in(mb).wait_send()

    @pl.when(section > 0)
    def _():
        for mb in range(micro):
            backward_in(mb).wait_send()


def layers(inputs, cotangent, gain, w_up, w_down):
    micro, toks, features = inputs.shape
    half, units, slab, jobs = features // 2, w_up.shape[1], SIDE * toks, 2 * micro
    core_rows, width = slab * SIDE, half // CHUNKS
    tokens = core_rows * CORES
    vmem = pl.BlockSpec(memory_space=pltpu.VMEM)
    hbm = pl.BlockSpec(memory_space=pl.ANY)
    dma = pltpu.SemaphoreType.DMA
    small = jax.ShapeDtypeStruct(inputs.shape, BF16)
    wide = jax.ShapeDtypeStruct((2, micro * tokens, half), BF16)
    narrow = jax.ShapeDtypeStruct((2, micro * tokens, units), BF16)
    return pl.pallas_call(
        layers_kernel,
        out_shape=(small, small, wide, wide, narrow, narrow),
        in_specs=[vmem, vmem, vmem, hbm, hbm],
        out_specs=(vmem, vmem, hbm, hbm, vmem, vmem),
        scratch_shapes=[
            pltpu.VMEM(w_up.shape, BF16),
            pltpu.VMEM(w_down.shape, BF16),
            pltpu.VMEM(inputs.shape, BF16),
            pltpu.VMEM(inputs.shape, BF16),
            pltpu.VMEM((jobs, 2, SIDE, toks, half), BF16),
            pltpu.VMEM((jobs, 2, tokens, half), BF16),
            pltpu.VMEM((2, CHUNKS, tokens, width), BF16),
            pltpu.VMEM((jobs, 2, CHUNKS, core_rows, width), BF16),
            pltpu.VMEM((jobs, 2, CHUNKS, core_rows, width), BF16),
            pltpu.VMEM((jobs, 2, CHUNKS, SIDE - 1, slab, width), BF16),
            pltpu.VMEM((jobs, 2, SIDE, toks, half), BF16),
            pltpu.VMEM((jobs, 2, SIDE - 1, toks, half), BF16),
            pltpu.VMEM((tokens, units), F32),
            pltpu.VMEM((tokens, units), F32),
            pltpu.VMEM((micro, tokens, units), F32),
            pltpu.VMEM((micro, tokens, units), F32),
            pltpu.VMEM((2, slab, half), F32),
            dma((2,)),
            dma((jobs, 2)),
            dma((2, micro)),
            dma((2, micro)),
            dma((jobs, 2)),
            dma((jobs, 2)),
            dma((jobs, 2)),
            dma((jobs, 2, SIDE - 1)),
            dma((jobs, 2)),
            dma((jobs, 2)),
            dma((jobs, 2, CHUNKS)),
            dma((jobs, 2, CHUNKS)),
            dma((jobs, 2, CHUNKS)),
            dma((jobs, 2, CHUNKS)),
            dma((jobs, 2)),
            dma((jobs, 2)),
        ],
        compiler_params=pltpu.CompilerParams(
            collective_id=0, has_side_effects=True, vmem_limit_bytes=VMEM_LIMIT
        ),
    )(inputs, cotangent, gain, w_up, w_down)


def shards(
    inputs, cotangent, gains, up_blocks, up_index, up_count, down_blocks, down_index, down_count
):
    features = inputs.shape[2]
    row_blocks = features // BLOCK
    group_blocks = FF // lax.axis_size("tp") // BLOCK
    w_up = densify(up_blocks[0], up_index[0], up_count[0, 0], row_blocks, group_blocks)
    w_down = densify(down_blocks[0], down_index[0], down_count[0, 0], group_blocks, row_blocks)
    outs, grads, normed, grad_rows, hidden, up_grad = layers(inputs, cotangent, gains, w_up, w_down)
    up_grads = weight_grad(normed, up_grad, up_index[0], up_count[0], True, group_blocks)
    down_grads = weight_grad(hidden, grad_rows, down_index[0], down_count[0], False, row_blocks)
    return (
        outs[None],
        grads[None],
        up_grads[None],
        down_grads[None],
    )


def solution(mesh):
    return jax.shard_map(
        shards,
        mesh=mesh,
        in_specs=(
            P(None, "tp", None),
            P(None, "tp", None),
            P("section", None),
            P("section", "tp", None),
            P("section", "tp"),
            P("section", "tp"),
            P("section", "tp", None),
            P("section", "tp"),
            P("section", "tp"),
        ),
        out_specs=(
            P("section", None, "tp", None),
            P("section", None, "tp", None),
            P("section", "tp", None),
            P("section", "tp", None),
        ),
        check_vma=False,
    )
```

```python
import functools

import jax
import jax.numpy as jnp
from jax import lax
from jax.experimental import pallas as pl
from jax.experimental.pallas import tpu as pltpu
from jax.sharding import PartitionSpec as P

FF = 16384
BLOCK = 64
NORM_EPSILON = 1e-05
MESH = pl.DeviceIdType.MESH
F32 = jnp.float32
BF16 = jnp.bfloat16
SIDE = 4
CORES = 2


LINES = BLOCK * BLOCK // 128
GROUP = 16
VMEM_LIMIT = 60 << 20
TILE = 2048
PAIRS = 32


def low_half(shape):
    return lax.broadcasted_iota(jnp.int32, shape, 1) < BLOCK


def place_kernel(slots_ref, blocks_ref, out_ref, lines, mixed, *, row_major, row_blocks, col_blocks):
    step = pl.program_id(0)

    @pl.when(step == 0)
    def _():
        @pl.loop(0, blocks_ref.shape[0] // (2 * GROUP))
        def _(t):
            for u in range(2):
                g = 2 * t + u
                rows = pl.ds(pl.multiple_of(g * GROUP, GROUP), GROUP)
                for k in range(LINES):
                    lines[pl.ds(pl.multiple_of((g * LINES + k) * GROUP, GROUP), GROUP), :] = blocks_ref[
                        rows, 128 * k : 128 * (k + 1)
                    ].astype(F32)

    low = low_half((LINES, 128))

    def block(place):
        slot = slots_ref[place]
        used = jnp.maximum(slot, 0)
        first = lax.div(used, GROUP) * (GROUP * LINES) + lax.rem(used, GROUP)
        value = lines[pl.ds(first, LINES, stride=GROUP), :]
        return jnp.where(slot >= 0, value, jnp.zeros_like(value))

    def pair(place, n):
        a, b = block(place), block(place + 1)
        mixed[pl.ds(n * BLOCK, LINES, stride=2), :] = jnp.where(low, a, pltpu.roll(b, BLOCK, 1))
        mixed[pl.ds(n * BLOCK + 1, LINES, stride=2), :] = jnp.where(low, pltpu.roll(a, BLOCK, 1), b)

    short = min(row_blocks, col_blocks)
    pairs = mixed.shape[0] // BLOCK

    def dense(n):
        return mixed[n * BLOCK : (n + 1) * BLOCK, :].astype(BF16)

    if row_major:
        rows = out_ref.shape[0] // BLOCK
        across = short // 2
        down = pairs // across

        @pl.loop(0, rows // down)
        def _(t):
            for n in range(pairs):
                pair((step * rows + t * down + n // across) * col_blocks + 2 * (n % across), n)
            for n in range(pairs):
                out_ref[
                    pl.ds(pl.multiple_of((t * down + n // across) * BLOCK, BLOCK), BLOCK),
                    (n % across) * 128 : (n % across + 1) * 128,
                ] = dense(n)
    else:
        cols = out_ref.shape[1] // 128
        across = pairs // short

        @pl.loop(0, cols // across)
        def _(t):
            for n in range(pairs):
                pair((n % short) * col_blocks + (step * cols + t * across + n // short) * 2, n)
            for n in range(pairs):
                out_ref[
                    (n % short) * BLOCK : (n % short + 1) * BLOCK,
                    pl.ds(pl.multiple_of((t * across + n // short) * 128, 128), 128),
                ] = dense(n)


def densify(blocks, block_index, live_count, row_blocks, col_blocks):
    slot_count = blocks.shape[0]
    slots = jnp.arange(slot_count, dtype=jnp.int32)
    places = jnp.arange(row_blocks * col_blocks, dtype=jnp.int32)
    hit = (block_index[None, :] == places[:, None]) & (slots < live_count)[None, :]
    slot_of_place = jnp.max(jnp.where(hit, slots[None, :], -1), axis=1)
    row_major = row_blocks > col_blocks
    steps = 8
    rows, cols = row_blocks * BLOCK, col_blocks * BLOCK
    if row_major:
        out_spec = pl.BlockSpec((rows // steps, cols), lambda i, *_: (i, 0))
    else:
        out_spec = pl.BlockSpec((rows, cols // steps), lambda i, *_: (0, i))
    return pl.pallas_call(
        functools.partial(place_kernel, row_major=row_major, row_blocks=row_blocks, col_blocks=col_blocks),
        out_shape=jax.ShapeDtypeStruct((rows, cols), blocks.dtype),
        grid_spec=pltpu.PrefetchScalarGridSpec(
            num_scalar_prefetch=1,
            grid=(steps,),
            in_specs=[pl.BlockSpec(blocks.shape, lambda i, *_: (0, 0), pipeline_mode=pl.Buffered(1))],
            out_specs=out_spec,
            scratch_shapes=[
                pltpu.VMEM((slot_count * LINES, 128), F32),
                pltpu.VMEM((PAIRS * BLOCK, 128), F32),
            ],
        ),
        compiler_params=pltpu.CompilerParams(vmem_limit_bytes=VMEM_LIMIT),
    )(slot_of_place, blocks)


def weight_grad_kernel(index_ref, count_ref, lhs_ref, rhs_ref, out_ref, dense, lines, *, up, col_blocks):
    step = pl.program_id(0)
    product = lax.dot_general(lhs_ref[0], rhs_ref[0], (((0,), (0,)), ((), ())), preferred_element_type=F32)
    height, width = product.shape
    chunks = width // 128
    column = height * pl.num_programs(0) if up else height
    for j in range(chunks):
        first = j * column + step * height if up else (step * chunks + j) * column
        dense[pl.ds(pl.multiple_of(first, 128), height), :] = product[:, 128 * j : 128 * (j + 1)]

    @pl.when(step == pl.num_programs(0) - 1)
    def _():
        count = count_ref[0]
        low = low_half((LINES, 128))

        @pl.loop(0, out_ref.shape[0] // GROUP)
        def _(g):
            for i in range(GROUP):
                slot = g * GROUP + i
                place = index_ref[slot]
                block_row, block_col = lax.div(place, col_blocks), lax.rem(place, col_blocks)
                first = lax.div(block_col, 2) * column + block_row * BLOCK
                odd = lax.rem(block_col, 2)
                even_rows = dense[pl.ds(first, LINES, stride=2), :]
                odd_rows = dense[pl.ds(first + 1, LINES, stride=2), :]
                value = jnp.where(
                    low,
                    jnp.where(odd == 1, pltpu.roll(even_rows, BLOCK, 1), even_rows),
                    jnp.where(odd == 1, odd_rows, pltpu.roll(odd_rows, BLOCK, 1)),
                )
                lines[pl.ds(i, LINES, stride=GROUP), :] = jnp.where(slot < count, value, jnp.zeros_like(value))
            rows = pl.ds(pl.multiple_of(g * GROUP, GROUP), GROUP)
            for k in range(LINES):
                out_ref[rows, 128 * k : 128 * (k + 1)] = lines[k * GROUP : (k + 1) * GROUP, :].astype(BF16)


def weight_grad(lhs, rhs, block_index, live_count, up, col_blocks):
    halves, tokens, width = (lhs if up else rhs).shape
    units = (rhs if up else lhs).shape[2]
    tile = TILE
    per_half = width // tile
    wide = pl.BlockSpec((1, tokens, tile), lambda i, *_: (i // per_half, 0, i % per_half))
    narrow = pl.BlockSpec((1, tokens, units), lambda i, *_: (i // per_half, 0, 0))
    slots = block_index.shape[0]
    return pl.pallas_call(
        functools.partial(weight_grad_kernel, up=up, col_blocks=col_blocks),
        out_shape=jax.ShapeDtypeStruct((slots, BLOCK * BLOCK), BF16),
        grid_spec=pltpu.PrefetchScalarGridSpec(
            num_scalar_prefetch=2,
            grid=(halves * per_half,),
            in_specs=[wide, narrow] if up else [narrow, wide],
            out_specs=pl.BlockSpec((slots, BLOCK * BLOCK), lambda i, *_: (0, 0), pipeline_mode=pl.Buffered(1)),
            scratch_shapes=[
                pltpu.VMEM((units * halves * width // 128, 128), F32),
                pltpu.VMEM((LINES * GROUP, 128), F32),
            ],
        ),
        compiler_params=pltpu.CompilerParams(vmem_limit_bytes=VMEM_LIMIT),
    )(block_index, live_count, lhs, rhs)


CHUNKS = 2


def layers_kernel(
    inp, cot, gain_ref, w_up_hbm, w_down_hbm,
    outs, grads, normed_hbm, grad_hbm, hid_out, ug_out,
    w_up, w_down, xin, gin, ibuf, gath, part, xbuf, sbuf, obuf, rsend, rbuf, ya, yb, up_keep, act_keep, tmp,
    w_sem, keep_sem, sec_send, sec_recv, p1_send, p1_recv, p2_send, p2_recv, sib_send, sib_recv,
    r0_send, r0_recv, r1_send, r1_recv, r2_send, r2_recv,
):
    micro, toks, features = inp.shape
    half = features // 2
    width = half // CHUNKS
    slab = SIDE * toks
    core_rows = SIDE * slab
    tokens = CORES * core_rows
    section, tp = lax.axis_index("section"), lax.axis_index("tp")
    sections = lax.axis_size("section")
    core = lax.rem(tp, CORES)
    y = lax.rem(lax.div(tp, CORES), SIDE)
    z = lax.div(tp, CORES * SIDE)
    sibling = {"tp": tp + 1 - 2 * core}
    inner = (z, y)
    outer = (y, z)
    SENDING, WAITING = (2, 1, 3), (1, 3, 2)

    def at(zz, yy):
        return {"tp": (zz * SIDE + yy) * CORES + core}

    def inner_peer(h, k):
        i = lax.rem(inner[h] + k, SIDE)
        return i, (at(i, y) if h == 0 else at(z, i))

    def outer_peer(h, k):
        o = lax.rem(outer[h] + k, SIDE)
        return o, (at(z, o) if h == 0 else at(o, y))

    def remote(src, dst, send, recv, device):
        return pltpu.make_async_remote_copy(
            src_ref=src, dst_ref=dst, send_sem=send, recv_sem=recv, device_id=device, device_id_type=MESH
        )

    load_up = pltpu.make_async_copy(w_up_hbm, w_up, w_sem.at[0])
    load_down = pltpu.make_async_copy(w_down_hbm, w_down, w_sem.at[1])
    load_up.start()
    load_down.start()

    barrier = pltpu.get_barrier_semaphore()
    peers = [sibling]
    for h in range(2):
        peers += [inner_peer(h, k)[1] for k in range(1, SIDE)]
    for peer in peers:
        pl.semaphore_signal(barrier, inc=1, device_id=peer, device_id_type=MESH)

    @pl.when(section > 0)
    def _():
        pl.semaphore_signal(barrier, inc=1, device_id={"section": section - 1}, device_id_type=MESH)

    @pl.when(section < sections - 1)
    def _():
        pl.semaphore_signal(barrier, inc=1, device_id={"section": section + 1}, device_id_type=MESH)

    @pl.when((section == 0) | (section == sections - 1))
    def _():
        pl.semaphore_wait(barrier, len(peers) + 1)

    @pl.when((section > 0) & (section < sections - 1))
    def _():
        pl.semaphore_wait(barrier, len(peers) + 2)

    def core_slabs(c):
        return pl.ds(pl.multiple_of(c * core_rows, core_rows), core_rows)

    def slab_rows(o, c):
        return pl.ds(pl.multiple_of((c * SIDE + o) * slab, slab), slab)

    def first_copies(job, h):
        ref = ibuf.at[job, h, pl.ds(0, SIDE - 1)]
        return remote(ref, ref, p1_send.at[job, h], p1_recv.at[job, h], sibling)

    def second_sends(job, h):
        ref = gath.at[job, h, pl.ds(0, (SIDE - 1) * slab)]
        return remote(ref, ref, p2_send.at[job, h], p2_recv.at[job, h, 0], sibling)

    def sibling_copies(job, h):
        ref = gath.at[job, h, core_slabs(1 - core)]
        return remote(ref, ref, sib_send.at[job, h], sib_recv.at[job, h], sibling)

    def exchange(job, h, q):
        return remote(
            part.at[h, q, core_slabs(1 - core)],
            xbuf.at[job, h, q],
            r0_send.at[job, h, q],
            r0_recv.at[job, h, q],
            sibling,
        )

    def outer_copies(job, h, q):
        ref = obuf.at[job, h, q]
        return remote(ref, ref, r1_send.at[job, h, q], r1_recv.at[job, h, q], sibling)

    def inner_copies(job, h):
        ref = rbuf.at[job, h]
        return remote(ref, ref, r2_send.at[job, h], r2_recv.at[job, h], sibling)

    def second_copy(job, h, k):
        mine = gath.at[job, h, slab_rows(outer[h], core)]
        return remote(mine, mine, p2_send.at[job, h], p2_recv.at[job, h, k - 1], outer_peer(h, k)[1])

    def gather_first(job, values):
        for h in range(2):
            mine = ibuf.at[job, h, inner[h]]
            mine[...] = values[:, h * half : (h + 1) * half].astype(BF16)
            for k in SENDING:
                remote(mine, mine, p1_send.at[job, h], p1_recv.at[job, h], inner_peer(h, k)[1]).start()

    def gather_second(job):
        for h in range(2):
            first_copies(job, h).wait_recv()
            for i in range(SIDE):
                tmp[h, i * toks : (i + 1) * toks, :] = ibuf[job, h, i].astype(F32)
            rows = slab_rows(outer[h], core)
            gath[job, h, rows, :] = tmp[h].astype(BF16)
            mine = gath.at[job, h, rows]
            for k in SENDING:
                second_copy(job, h, k).start()
            remote(mine, mine, sib_send.at[job, h], sib_recv.at[job, h], sibling).start()

    def gather_third(job):
        for k in WAITING:
            for h in range(2):
                second_copy(job, h, k).wait_recv()
                came = gath.at[job, h, slab_rows(outer_peer(h, SIDE - k)[0], core)]
                remote(came, came, sib_send.at[job, h], sib_recv.at[job, h], sibling).start()

    def keep(job, mb, rows_hbm):
        return [
            pltpu.make_async_copy(
                gath.at[job, h],
                rows_hbm.at[h, pl.ds(pl.multiple_of(mb * tokens, tokens), tokens)],
                keep_sem.at[job, h],
            )
            for h in range(2)
        ]

    def permuted(target, source, add):
        for c in range(CORES):
            for a in range(SIDE):
                for b in range(SIDE):
                    to, of = ((c * SIDE + a) * SIDE + b) * toks, ((c * SIDE + b) * SIDE + a) * toks
                    moved = source[of : of + toks, :]
                    target[to : to + toks, :] = target[to : to + toks, :] + moved if add else moved

    def scatter(job, product, meanwhile):
        def spread(h, q):
            exchange(job, h, q).wait_recv()
            sbuf[job, h, q] = part[h, q, core_slabs(core), :] + xbuf[job, h, q]
            for k in SENDING:
                o, peer = outer_peer(h, k)
                remote(
                    sbuf.at[job, h, q, pl.ds(pl.multiple_of(o * slab, slab), slab)],
                    obuf.at[job, h, q, k - 1],
                    r1_send.at[job, h, q],
                    r1_recv.at[job, h, q],
                    peer,
                ).start()

        steps = [(h, q) for q in range(CHUNKS) for h in range(2)]
        for n, (h, q) in enumerate(steps):
            part[h, q] = product(h, q).astype(BF16)
            exchange(job, h, q).start()
            if n:
                spread(*steps[n - 1])
        spread(*steps[-1])
        for h in range(2):
            for q in range(CHUNKS):
                outer_copies(job, h, q).wait_recv()
                own = sbuf[job, h, q, pl.ds(pl.multiple_of(outer[h] * slab, slab), slab), :].astype(F32)
                came = [obuf[job, h, q, k].astype(F32) for k in range(SIDE - 1)]
                tmp[h, :, q * width : (q + 1) * width] = own + (came[0] + came[1] + came[2])
            for i in range(SIDE):
                rsend[job, h, i] = tmp[h, i * toks : (i + 1) * toks, :].astype(BF16)
            for k in SENDING:
                i, peer = inner_peer(h, k)
                remote(
                    rsend.at[job, h, i], rbuf.at[job, h, k - 1], r2_send.at[job, h], r2_recv.at[job, h], peer
                ).start()
        meanwhile()
        for h, q in steps:
            exchange(job, h, q).wait_send()
        sums = []
        for h in range(2):
            inner_copies(job, h).wait_recv()
            came = [rbuf[job, h, k].astype(F32) for k in range(SIDE - 1)]
            sums.append(rsend[job, h, inner[h]].astype(F32) + (came[0] + came[1] + came[2]))
        return jnp.concatenate(sums, axis=1)

    gain = gain_ref[...].astype(F32)
    NT = (((1,), (1,)), ((), ()))

    def columns(h, q=0, size=half):
        return slice(h * half + q * size, h * half + (q + 1) * size)

    def forward_in(mb):
        return remote(outs.at[mb], xin.at[mb], sec_send.at[0, mb], sec_recv.at[0, mb], {"section": section + 1})

    def backward_in(mb):
        return remote(grads.at[mb], gin.at[mb], sec_send.at[1, mb], sec_recv.at[1, mb], {"section": section - 1})

    def norm(mb):
        values = xin[mb].astype(F32)
        inv_rms = lax.rsqrt(jnp.mean(values * values, axis=-1, keepdims=True) + NORM_EPSILON)
        return values, inv_rms

    def begin_forward(mb):
        @pl.when(section == 0)
        def _():
            xin[mb] = inp[mb]

        @pl.when(section > 0)
        def _():
            forward_in(mb).wait_recv()

        values, inv_rms = norm(mb)
        gather_first(mb, values * inv_rms * gain)

    def forward(mb, _):
        job = mb
        gather_third(job)

        @pl.when((mb == 0) & (section < sections - 1))
        def _():
            load_up.wait()
            load_down.wait()

        for h, acc in ((0, ya), (1, yb)):
            sibling_copies(job, h).wait_recv()
            acc[...] = jnp.dot(gath[job, h], w_up[columns(h), :], preferred_element_type=F32)

        permuted(ya, yb, True)
        up = ya[...]
        up_keep[mb] = up
        hidden = up / (1.0 + jnp.exp(-up))
        ya[...] = hidden
        permuted(yb, ya, False)
        kept = pl.ds(pl.multiple_of(mb * tokens, tokens), tokens)
        for h, acc in ((0, ya), (1, yb)):
            hid_out[h, kept, :] = acc[...].astype(BF16)

        def product(h, q):
            return jnp.dot(hid_out[h, kept, :], w_down[:, columns(h, q, width)], preferred_element_type=F32)

        def meanwhile():
            @pl.when(mb < micro - 1)
            def _():
                begin_forward(mb + 1)

        mixed = scatter(job, product, meanwhile)
        outs[mb] = (xin[mb].astype(F32) + mixed).astype(BF16)

        @pl.when(section < sections - 1)
        def _():
            forward_in(mb).start()

        @pl.when(mb < micro - 1)
        def _():
            gather_second(job + 1)

        for copy in keep(job, mb, normed_hbm):
            copy.start()
        return 0

    def hidden_grad(mb):
        job = micro + mb
        gather_third(job)
        for h, acc in ((0, ya), (1, yb)):
            sibling_copies(job, h).wait_recv()
            acc[...] = lax.dot_general(gath[job, h], w_down[:, columns(h)], NT, preferred_element_type=F32)
        for copy in keep(job, mb, grad_hbm):
            copy.start()
        permuted(ya, yb, True)
        act_keep[mb] = ya[...]

    def begin_backward(mb):
        backward_in(mb).wait_recv()
        gather_first(micro + mb, gin[mb].astype(F32))

    def backward(mb, _):
        job = micro + mb

        @pl.when(section < sections - 1)
        def _():
            hidden_grad(mb)

        up = up_keep[mb]
        q = 1.0 / (1.0 + jnp.exp(-up))
        ya[...] = act_keep[mb] * q * (1.0 + up * (1.0 - q))
        permuted(yb, ya, False)
        kept = pl.ds(pl.multiple_of(mb * tokens, tokens), tokens)
        for h, acc in ((0, ya), (1, yb)):
            ug_out[h, kept, :] = acc[...].astype(BF16)

        def product(h, q):
            return lax.dot_general(ug_out[h, kept, :], w_up[columns(h, q, width), :], NT, preferred_element_type=F32)

        more = (mb < micro - 1) & (section < sections - 1)

        def meanwhile():
            @pl.when(more)
            def _():
                begin_backward(mb + 1)

        scaled = scatter(job, product, meanwhile) * gain
        values, inv_rms = norm(mb)
        term = inv_rms * scaled - values * (inv_rms * inv_rms * inv_rms) * jnp.mean(
            scaled * values, axis=-1, keepdims=True
        )
        grads[mb] = (gin[mb].astype(F32) + term).astype(BF16)

        @pl.when(section > 0)
        def _():
            backward_in(mb).start()

        @pl.when(more)
        def _():
            gather_second(job + 1)

        return 0

    @pl.when(section == sections - 1)
    def _():
        load_up.wait()
        load_down.wait()
        gin[...] = cot[...]

        @pl.loop(0, micro)
        def _(mb):
            gather_first(micro + mb, gin[mb].astype(F32))
            gather_second(micro + mb)
            hidden_grad(mb)

    begin_forward(0)
    gather_second(0)
    lax.fori_loop(0, micro, forward, 0)

    @pl.when(section < sections - 1)
    def _():
        begin_backward(0)
        gather_second(micro)

    lax.fori_loop(0, micro, backward, 0)

    for mb in range(micro):
        for copy in keep(mb, mb, normed_hbm) + keep(micro + mb, mb, grad_hbm):
            copy.wait()
    for job in range(2 * micro):
        for h in range(2):
            for copies in (first_copies, second_sends, sibling_copies, inner_copies):
                copies(job, h).wait_send()
            for q in range(CHUNKS):
                outer_copies(job, h, q).wait_send()

    @pl.when(section < sections - 1)
    def _():
        for mb in range(micro):
            forward_in(mb).wait_send()

    @pl.when(section > 0)
    def _():
        for mb in range(micro):
            backward_in(mb).wait_send()


def layers(inputs, cotangent, gain, w_up, w_down):
    micro, toks, features = inputs.shape
    half, units, slab, jobs = features // 2, w_up.shape[1], SIDE * toks, 2 * micro
    core_rows, width = slab * SIDE, half // CHUNKS
    tokens = core_rows * CORES
    vmem = pl.BlockSpec(memory_space=pltpu.VMEM)
    hbm = pl.BlockSpec(memory_space=pl.ANY)
    dma = pltpu.SemaphoreType.DMA
    small = jax.ShapeDtypeStruct(inputs.shape, BF16)
    wide = jax.ShapeDtypeStruct((2, micro * tokens, half), BF16)
    narrow = jax.ShapeDtypeStruct((2, micro * tokens, units), BF16)
    return pl.pallas_call(
        layers_kernel,
        out_shape=(small, small, wide, wide, narrow, narrow),
        in_specs=[vmem, vmem, vmem, hbm, hbm],
        out_specs=(vmem, vmem, hbm, hbm, vmem, vmem),
        scratch_shapes=[
            pltpu.VMEM(w_up.shape, BF16),
            pltpu.VMEM(w_down.shape, BF16),
            pltpu.VMEM(inputs.shape, BF16),
            pltpu.VMEM(inputs.shape, BF16),
            pltpu.VMEM((jobs, 2, SIDE, toks, half), BF16),
            pltpu.VMEM((jobs, 2, tokens, half), BF16),
            pltpu.VMEM((2, CHUNKS, tokens, width), BF16),
            pltpu.VMEM((jobs, 2, CHUNKS, core_rows, width), BF16),
            pltpu.VMEM((jobs, 2, CHUNKS, core_rows, width), BF16),
            pltpu.VMEM((jobs, 2, CHUNKS, SIDE - 1, slab, width), BF16),
            pltpu.VMEM((jobs, 2, SIDE, toks, half), BF16),
            pltpu.VMEM((jobs, 2, SIDE - 1, toks, half), BF16),
            pltpu.VMEM((tokens, units), F32),
            pltpu.VMEM((tokens, units), F32),
            pltpu.VMEM((micro, tokens, units), F32),
            pltpu.VMEM((micro, tokens, units), F32),
            pltpu.VMEM((2, slab, half), F32),
            dma((2,)),
            dma((jobs, 2)),
            dma((2, micro)),
            dma((2, micro)),
            dma((jobs, 2)),
            dma((jobs, 2)),
            dma((jobs, 2)),
            dma((jobs, 2, SIDE - 1)),
            dma((jobs, 2)),
            dma((jobs, 2)),
            dma((jobs, 2, CHUNKS)),
            dma((jobs, 2, CHUNKS)),
            dma((jobs, 2, CHUNKS)),
            dma((jobs, 2, CHUNKS)),
            dma((jobs, 2)),
            dma((jobs, 2)),
        ],
        compiler_params=pltpu.CompilerParams(
            collective_id=0, has_side_effects=True, vmem_limit_bytes=VMEM_LIMIT
        ),
    )(inputs, cotangent, gain, w_up, w_down)


def shards(
    inputs, cotangent, gains, up_blocks, up_index, up_count, down_blocks, down_index, down_count
):
    features = inputs.shape[2]
    row_blocks = features // BLOCK
    group_blocks = FF // lax.axis_size("tp") // BLOCK
    w_up = densify(up_blocks[0], up_index[0], up_count[0, 0], row_blocks, group_blocks)
    w_down = densify(down_blocks[0], down_index[0], down_count[0, 0], group_blocks, row_blocks)
    outs, grads, normed, grad_rows, hidden, up_grad = layers(inputs, cotangent, gains, w_up, w_down)
    up_grads = weight_grad(normed, up_grad, up_index[0], up_count[0], True, group_blocks)
    down_grads = weight_grad(hidden, grad_rows, down_index[0], down_count[0], False, row_blocks)
    return (
        outs[None],
        grads[None],
        up_grads[None],
        down_grads[None],
    )


def solution(mesh):
    return jax.shard_map(
        shards,
        mesh=mesh,
        in_specs=(
            P(None, "tp", None),
            P(None, "tp", None),
            P("section", None),
            P("section", "tp", None),
            P("section", "tp"),
            P("section", "tp"),
            P("section", "tp", None),
            P("section", "tp"),
            P("section", "tp"),
        ),
        out_specs=(
            P("section", None, "tp", None),
            P("section", None, "tp", None),
            P("section", "tp", None),
            P("section", "tp", None),
        ),
        check_vma=False,
    )
```

```python
import functools

import jax
import jax.numpy as jnp
from jax import lax
from jax.experimental import pallas as pl
from jax.experimental.pallas import tpu as pltpu
from jax.sharding import PartitionSpec as P

FF = 16384
BLOCK = 64
NORM_EPSILON = 1e-05
MESH = pl.DeviceIdType.MESH
F32 = jnp.float32
BF16 = jnp.bfloat16
SIDE = 4
CORES = 2


LINES = BLOCK * BLOCK // 128
GROUP = 16
VMEM_LIMIT = 60 << 20
TILE = 2048
PAIRS = 32


def low_half(shape):
    return lax.broadcasted_iota(jnp.int32, shape, 1) < BLOCK


def place_kernel(slots_ref, blocks_ref, out_ref, lines, mixed, *, row_major, row_blocks, col_blocks):
    step = pl.program_id(0)

    @pl.when(step == 0)
    def _():
        @pl.loop(0, blocks_ref.shape[0] // (2 * GROUP))
        def _(t):
            for u in range(2):
                g = 2 * t + u
                rows = pl.ds(pl.multiple_of(g * GROUP, GROUP), GROUP)
                for k in range(LINES):
                    lines[pl.ds(pl.multiple_of((g * LINES + k) * GROUP, GROUP), GROUP), :] = blocks_ref[
                        rows, 128 * k : 128 * (k + 1)
                    ].astype(F32)

    low = low_half((LINES, 128))

    def block(place):
        slot = slots_ref[place]
        used = jnp.maximum(slot, 0)
        first = lax.div(used, GROUP) * (GROUP * LINES) + lax.rem(used, GROUP)
        value = lines[pl.ds(first, LINES, stride=GROUP), :]
        return jnp.where(slot >= 0, value, jnp.zeros_like(value))

    def pair(place, n):
        a, b = block(place), block(place + 1)
        mixed[pl.ds(n * BLOCK, LINES, stride=2), :] = jnp.where(low, a, pltpu.roll(b, BLOCK, 1))
        mixed[pl.ds(n * BLOCK + 1, LINES, stride=2), :] = jnp.where(low, pltpu.roll(a, BLOCK, 1), b)

    short = min(row_blocks, col_blocks)
    pairs = mixed.shape[0] // BLOCK

    def dense(n):
        return mixed[n * BLOCK : (n + 1) * BLOCK, :].astype(BF16)

    if row_major:
        rows = out_ref.shape[0] // BLOCK
        across = short // 2
        down = pairs // across

        @pl.loop(0, rows // down)
        def _(t):
            for n in range(pairs):
                pair((step * rows + t * down + n // across) * col_blocks + 2 * (n % across), n)
            for n in range(pairs):
                out_ref[
                    pl.ds(pl.multiple_of((t * down + n // across) * BLOCK, BLOCK), BLOCK),
                    (n % across) * 128 : (n % across + 1) * 128,
                ] = dense(n)
    else:
        cols = out_ref.shape[1] // 128
        across = pairs // short

        @pl.loop(0, cols // across)
        def _(t):
            for n in range(pairs):
                pair((n % short) * col_blocks + (step * cols + t * across + n // short) * 2, n)
            for n in range(pairs):
                out_ref[
                    (n % short) * BLOCK : (n % short + 1) * BLOCK,
                    pl.ds(pl.multiple_of((t * across + n // short) * 128, 128), 128),
                ] = dense(n)


def densify(blocks, block_index, live_count, row_blocks, col_blocks):
    slot_count = blocks.shape[0]
    slots = jnp.arange(slot_count, dtype=jnp.int32)
    places = jnp.arange(row_blocks * col_blocks, dtype=jnp.int32)
    hit = (block_index[None, :] == places[:, None]) & (slots < live_count)[None, :]
    slot_of_place = jnp.max(jnp.where(hit, slots[None, :], -1), axis=1)
    row_major = row_blocks > col_blocks
    steps = 8
    rows, cols = row_blocks * BLOCK, col_blocks * BLOCK
    if row_major:
        out_spec = pl.BlockSpec((rows // steps, cols), lambda i, *_: (i, 0))
    else:
        out_spec = pl.BlockSpec((rows, cols // steps), lambda i, *_: (0, i))
    return pl.pallas_call(
        functools.partial(place_kernel, row_major=row_major, row_blocks=row_blocks, col_blocks=col_blocks),
        out_shape=jax.ShapeDtypeStruct((rows, cols), blocks.dtype),
        grid_spec=pltpu.PrefetchScalarGridSpec(
            num_scalar_prefetch=1,
            grid=(steps,),
            in_specs=[pl.BlockSpec(blocks.shape, lambda i, *_: (0, 0), pipeline_mode=pl.Buffered(1))],
            out_specs=out_spec,
            scratch_shapes=[
                pltpu.VMEM((slot_count * LINES, 128), F32),
                pltpu.VMEM((PAIRS * BLOCK, 128), F32),
            ],
        ),
        compiler_params=pltpu.CompilerParams(vmem_limit_bytes=VMEM_LIMIT),
    )(slot_of_place, blocks)


def weight_grad_kernel(index_ref, count_ref, lhs_ref, rhs_ref, out_ref, dense, lines, *, up, col_blocks):
    step = pl.program_id(0)
    product = lax.dot_general(lhs_ref[0], rhs_ref[0], (((0,), (0,)), ((), ())), preferred_element_type=F32)
    height, width = product.shape
    chunks = width // 128
    column = height * pl.num_programs(0) if up else height
    for j in range(chunks):
        first = j * column + step * height if up else (step * chunks + j) * column
        dense[pl.ds(pl.multiple_of(first, 128), height), :] = product[:, 128 * j : 128 * (j + 1)]

    @pl.when(step == pl.num_programs(0) - 1)
    def _():
        count = count_ref[0]
        low = low_half((LINES, 128))

        @pl.loop(0, out_ref.shape[0] // GROUP)
        def _(g):
            for i in range(GROUP):
                slot = g * GROUP + i
                place = index_ref[slot]
                block_row, block_col = lax.div(place, col_blocks), lax.rem(place, col_blocks)
                first = lax.div(block_col, 2) * column + block_row * BLOCK
                odd = lax.rem(block_col, 2)
                even_rows = dense[pl.ds(first, LINES, stride=2), :]
                odd_rows = dense[pl.ds(first + 1, LINES, stride=2), :]
                value = jnp.where(
                    low,
                    jnp.where(odd == 1, pltpu.roll(even_rows, BLOCK, 1), even_rows),
                    jnp.where(odd == 1, odd_rows, pltpu.roll(odd_rows, BLOCK, 1)),
                )
                lines[pl.ds(i, LINES, stride=GROUP), :] = jnp.where(slot < count, value, jnp.zeros_like(value))
            rows = pl.ds(pl.multiple_of(g * GROUP, GROUP), GROUP)
            for k in range(LINES):
                out_ref[rows, 128 * k : 128 * (k + 1)] = lines[k * GROUP : (k + 1) * GROUP, :].astype(BF16)


def weight_grad(lhs, rhs, block_index, live_count, up, col_blocks):
    halves, tokens, width = (lhs if up else rhs).shape
    units = (rhs if up else lhs).shape[2]
    tile = TILE
    per_half = width // tile
    wide = pl.BlockSpec((1, tokens, tile), lambda i, *_: (i // per_half, 0, i % per_half))
    narrow = pl.BlockSpec((1, tokens, units), lambda i, *_: (i // per_half, 0, 0))
    slots = block_index.shape[0]
    return pl.pallas_call(
        functools.partial(weight_grad_kernel, up=up, col_blocks=col_blocks),
        out_shape=jax.ShapeDtypeStruct((slots, BLOCK * BLOCK), BF16),
        grid_spec=pltpu.PrefetchScalarGridSpec(
            num_scalar_prefetch=2,
            grid=(halves * per_half,),
            in_specs=[wide, narrow] if up else [narrow, wide],
            out_specs=pl.BlockSpec((slots, BLOCK * BLOCK), lambda i, *_: (0, 0), pipeline_mode=pl.Buffered(1)),
            scratch_shapes=[
                pltpu.VMEM((units * halves * width // 128, 128), F32),
                pltpu.VMEM((LINES * GROUP, 128), F32),
            ],
        ),
        compiler_params=pltpu.CompilerParams(vmem_limit_bytes=VMEM_LIMIT),
    )(block_index, live_count, lhs, rhs)


CHUNKS = 2


def layers_kernel(
    inp, cot, gain_ref, w_up_hbm, w_down_hbm,
    outs, grads, normed_hbm, grad_hbm, hid_out, ug_out,
    w_up, w_down, xin, gin, ibuf, gath, part, xbuf, sbuf, obuf, rsend, rbuf, ya, yb, up_keep, act_keep, inv_keep, tmp,
    w_sem, keep_sem, sec_send, sec_recv, p1_send, p1_recv, p2_send, p2_recv, sib_send, sib_recv,
    r0_send, r0_recv, r1_send, r1_recv, r2_send, r2_recv,
):
    micro, toks, features = inp.shape
    half = features // 2
    width = half // CHUNKS
    slab = SIDE * toks
    core_rows = SIDE * slab
    tokens = CORES * core_rows
    section, tp = lax.axis_index("section"), lax.axis_index("tp")
    sections = lax.axis_size("section")
    core = lax.rem(tp, CORES)
    y = lax.rem(lax.div(tp, CORES), SIDE)
    z = lax.div(tp, CORES * SIDE)
    sibling = {"tp": tp + 1 - 2 * core}
    inner = (z, y)
    outer = (y, z)
    SENDING, WAITING = (2, 1, 3), (1, 3, 2)

    def at(zz, yy):
        return {"tp": (zz * SIDE + yy) * CORES + core}

    def inner_peer(h, k):
        i = lax.rem(inner[h] + k, SIDE)
        return i, (at(i, y) if h == 0 else at(z, i))

    def outer_peer(h, k):
        o = lax.rem(outer[h] + k, SIDE)
        return o, (at(z, o) if h == 0 else at(o, y))

    def remote(src, dst, send, recv, device):
        return pltpu.make_async_remote_copy(
            src_ref=src, dst_ref=dst, send_sem=send, recv_sem=recv, device_id=device, device_id_type=MESH
        )

    load_up = pltpu.make_async_copy(w_up_hbm, w_up, w_sem.at[0])
    load_down = pltpu.make_async_copy(w_down_hbm, w_down, w_sem.at[1])
    load_up.start()
    load_down.start()

    barrier = pltpu.get_barrier_semaphore()
    peers = [sibling]
    for h in range(2):
        peers += [inner_peer(h, k)[1] for k in range(1, SIDE)]
    for peer in peers:
        pl.semaphore_signal(barrier, inc=1, device_id=peer, device_id_type=MESH)

    @pl.when(section > 0)
    def _():
        pl.semaphore_signal(barrier, inc=1, device_id={"section": section - 1}, device_id_type=MESH)

    @pl.when(section < sections - 1)
    def _():
        pl.semaphore_signal(barrier, inc=1, device_id={"section": section + 1}, device_id_type=MESH)

    @pl.when((section == 0) | (section == sections - 1))
    def _():
        pl.semaphore_wait(barrier, len(peers) + 1)

    @pl.when((section > 0) & (section < sections - 1))
    def _():
        pl.semaphore_wait(barrier, len(peers) + 2)

    def core_slabs(c):
        return pl.ds(pl.multiple_of(c * core_rows, core_rows), core_rows)

    def slab_rows(o, c):
        return pl.ds(pl.multiple_of((c * SIDE + o) * slab, slab), slab)

    def first_copies(job, h):
        ref = ibuf.at[job, h, pl.ds(0, SIDE - 1)]
        return remote(ref, ref, p1_send.at[job, h], p1_recv.at[job, h], sibling)

    def second_sends(job, h):
        ref = gath.at[job, h, pl.ds(0, (SIDE - 1) * slab)]
        return remote(ref, ref, p2_send.at[job, h], p2_recv.at[job, h, 0], sibling)

    def sibling_copies(job, h):
        ref = gath.at[job, h, core_slabs(1 - core)]
        return remote(ref, ref, sib_send.at[job, h], sib_recv.at[job, h], sibling)

    def exchange(job, h, q):
        return remote(
            part.at[h, q, core_slabs(1 - core)],
            xbuf.at[job, h, q],
            r0_send.at[job, h, q],
            r0_recv.at[job, h, q],
            sibling,
        )

    def outer_copies(job, h, q):
        ref = obuf.at[job, h, q]
        return remote(ref, ref, r1_send.at[job, h, q], r1_recv.at[job, h, q], sibling)

    def inner_copies(job, h):
        ref = rbuf.at[job, h]
        return remote(ref, ref, r2_send.at[job, h], r2_recv.at[job, h], sibling)

    def gather(job, values):
        for h in range(2):
            mine = ibuf.at[job, h, inner[h]]
            mine[...] = values[:, h * half : (h + 1) * half].astype(BF16)
            for k in SENDING:
                remote(mine, mine, p1_send.at[job, h], p1_recv.at[job, h], inner_peer(h, k)[1]).start()
        second = {}
        for h in range(2):
            first_copies(job, h).wait_recv()
            for i in range(SIDE):
                tmp[h, i * toks : (i + 1) * toks, :] = ibuf[job, h, i].astype(F32)
            rows = slab_rows(outer[h], core)
            gath[job, h, rows, :] = tmp[h].astype(BF16)
            mine = gath.at[job, h, rows]
            for k in SENDING:
                copy = remote(mine, mine, p2_send.at[job, h], p2_recv.at[job, h, k - 1], outer_peer(h, k)[1])
                copy.start()
                second[h, k] = copy
            remote(mine, mine, sib_send.at[job, h], sib_recv.at[job, h], sibling).start()
        for k in WAITING:
            for h in range(2):
                second[h, k].wait_recv()
                came = gath.at[job, h, slab_rows(outer_peer(h, SIDE - k)[0], core)]
                remote(came, came, sib_send.at[job, h], sib_recv.at[job, h], sibling).start()

    def keep(job, mb, rows_hbm):
        return [
            pltpu.make_async_copy(
                gath.at[job, h],
                rows_hbm.at[h, pl.ds(pl.multiple_of(mb * tokens, tokens), tokens)],
                keep_sem.at[job, h],
            )
            for h in range(2)
        ]

    def permuted(target, source, add):
        for c in range(CORES):
            for a in range(SIDE):
                for b in range(SIDE):
                    to, of = ((c * SIDE + a) * SIDE + b) * toks, ((c * SIDE + b) * SIDE + a) * toks
                    moved = source[of : of + toks, :]
                    target[to : to + toks, :] = target[to : to + toks, :] + moved if add else moved

    def scatter(job, product):
        def spread(h, q):
            exchange(job, h, q).wait_recv()
            sbuf[job, h, q] = part[h, q, core_slabs(core), :] + xbuf[job, h, q]
            for k in SENDING:
                o, peer = outer_peer(h, k)
                remote(
                    sbuf.at[job, h, q, pl.ds(pl.multiple_of(o * slab, slab), slab)],
                    obuf.at[job, h, q, k - 1],
                    r1_send.at[job, h, q],
                    r1_recv.at[job, h, q],
                    peer,
                ).start()

        steps = [(h, q) for q in range(CHUNKS) for h in range(2)]
        for n, (h, q) in enumerate(steps):
            part[h, q] = product(h, q).astype(BF16)
            exchange(job, h, q).start()
            if n:
                spread(*steps[n - 1])
        spread(*steps[-1])
        for h in range(2):
            for copies in (first_copies, second_sends, sibling_copies):
                copies(job, h).wait_send()
        for h in range(2):
            for q in range(CHUNKS):
                outer_copies(job, h, q).wait_recv()
                own = sbuf[job, h, q, pl.ds(pl.multiple_of(outer[h] * slab, slab), slab), :].astype(F32)
                came = [obuf[job, h, q, k].astype(F32) for k in range(SIDE - 1)]
                tmp[h, :, q * width : (q + 1) * width] = own + (came[0] + came[1] + came[2])
            for i in range(SIDE):
                rsend[job, h, i] = tmp[h, i * toks : (i + 1) * toks, :].astype(BF16)
            for k in SENDING:
                i, peer = inner_peer(h, k)
                remote(
                    rsend.at[job, h, i], rbuf.at[job, h, k - 1], r2_send.at[job, h], r2_recv.at[job, h], peer
                ).start()
        for h, q in steps:
            exchange(job, h, q).wait_send()
        sums = []
        for h in range(2):
            inner_copies(job, h).wait_recv()
            came = [rbuf[job, h, k].astype(F32) for k in range(SIDE - 1)]
            sums.append(rsend[job, h, inner[h]].astype(F32) + (came[0] + came[1] + came[2]))
        return jnp.concatenate(sums, axis=1)

    gain = gain_ref[...].astype(F32)
    NT = (((1,), (1,)), ((), ()))

    def columns(h, q=0, size=half):
        return slice(h * half + q * size, h * half + (q + 1) * size)

    def forward_in(mb):
        return remote(outs.at[mb], xin.at[mb], sec_send.at[0, mb], sec_recv.at[0, mb], {"section": section + 1})

    def backward_in(mb):
        return remote(grads.at[mb], gin.at[mb], sec_send.at[1, mb], sec_recv.at[1, mb], {"section": section - 1})

    def norm(mb):
        values = xin[mb].astype(F32)
        inv_rms = lax.rsqrt(jnp.mean(values * values, axis=-1, keepdims=True) + NORM_EPSILON)
        return values, inv_rms

    def forward(mb, _):
        job = mb

        @pl.when(section == 0)
        def _():
            xin[mb] = inp[mb]

        @pl.when(section > 0)
        def _():
            forward_in(mb).wait_recv()

        values, inv_rms = norm(mb)
        inv_keep[mb] = jnp.broadcast_to(inv_rms, inv_keep.shape[1:])
        gather(job, values * inv_rms * gain)

        @pl.when((mb == 0) & (section < sections - 1))
        def _():
            load_up.wait()
            load_down.wait()

        for h, acc in ((0, ya), (1, yb)):
            sibling_copies(job, h).wait_recv()
            acc[...] = jnp.dot(gath[job, h], w_up[columns(h), :], preferred_element_type=F32)

        permuted(ya, yb, True)
        up = ya[...]
        up_keep[mb] = up
        hidden = up / (1.0 + jnp.exp(-up))
        ya[...] = hidden
        permuted(yb, ya, False)
        kept = pl.ds(pl.multiple_of(mb * tokens, tokens), tokens)
        for h, acc in ((0, ya), (1, yb)):
            hid_out[h, kept, :] = acc[...].astype(BF16)

        def product(h, q):
            return jnp.dot(hid_out[h, kept, :], w_down[:, columns(h, q, width)], preferred_element_type=F32)

        mixed = scatter(job, product)
        outs[mb] = (xin[mb].astype(F32) + mixed).astype(BF16)

        @pl.when(section < sections - 1)
        def _():
            forward_in(mb).start()

        for copy in keep(job, mb, normed_hbm):
            copy.start()
        up = up_keep[mb]
        q = 1.0 / (1.0 + jnp.exp(-up))
        up_keep[mb] = q * (1.0 + up * (1.0 - q))
        return 0

    def hidden_grad(mb):
        job = micro + mb
        gather(job, gin[mb].astype(F32))
        for h, acc in ((0, ya), (1, yb)):
            sibling_copies(job, h).wait_recv()
            acc[...] = lax.dot_general(gath[job, h], w_down[:, columns(h)], NT, preferred_element_type=F32)
        for copy in keep(job, mb, grad_hbm):
            copy.start()
        permuted(ya, yb, True)
        act_keep[mb] = ya[...]

    def backward(mb, _):
        job = micro + mb

        @pl.when(section < sections - 1)
        def _():
            backward_in(mb).wait_recv()
            hidden_grad(mb)

        ya[...] = act_keep[mb] * up_keep[mb]
        permuted(yb, ya, False)
        kept = pl.ds(pl.multiple_of(mb * tokens, tokens), tokens)
        for h, acc in ((0, ya), (1, yb)):
            ug_out[h, kept, :] = acc[...].astype(BF16)

        def product(h, q):
            return lax.dot_general(ug_out[h, kept, :], w_up[columns(h, q, width), :], NT, preferred_element_type=F32)

        scaled = scatter(job, product) * gain
        values, inv_rms = xin[mb].astype(F32), inv_keep[mb][:, :1]
        term = inv_rms * scaled - values * (inv_rms * inv_rms * inv_rms) * jnp.mean(
            scaled * values, axis=-1, keepdims=True
        )
        grads[mb] = (gin[mb].astype(F32) + term).astype(BF16)

        @pl.when(section > 0)
        def _():
            backward_in(mb).start()

        return 0

    @pl.when(section == sections - 1)
    def _():
        load_up.wait()
        load_down.wait()
        gin[...] = cot[...]

        @pl.loop(0, micro)
        def _(mb):
            hidden_grad(mb)

    lax.fori_loop(0, micro, forward, 0)
    lax.fori_loop(0, micro, backward, 0)

    for mb in range(micro):
        for copy in keep(mb, mb, normed_hbm) + keep(micro + mb, mb, grad_hbm):
            copy.wait()
    for job in range(2 * micro):
        for h in range(2):
            inner_copies(job, h).wait_send()
            for q in range(CHUNKS):
                outer_copies(job, h, q).wait_send()

    @pl.when(section < sections - 1)
    def _():
        for mb in range(micro):
            forward_in(mb).wait_send()

    @pl.when(section > 0)
    def _():
        for mb in range(micro):
            backward_in(mb).wait_send()


def layers(inputs, cotangent, gain, w_up, w_down):
    micro, toks, features = inputs.shape
    half, units, slab, jobs = features // 2, w_up.shape[1], SIDE * toks, 2 * micro
    core_rows, width = slab * SIDE, half // CHUNKS
    tokens = core_rows * CORES
    vmem = pl.BlockSpec(memory_space=pltpu.VMEM)
    hbm = pl.BlockSpec(memory_space=pl.ANY)
    dma = pltpu.SemaphoreType.DMA
    small = jax.ShapeDtypeStruct(inputs.shape, BF16)
    wide = jax.ShapeDtypeStruct((2, micro * tokens, half), BF16)
    narrow = jax.ShapeDtypeStruct((2, micro * tokens, units), BF16)
    return pl.pallas_call(
        layers_kernel,
        out_shape=(small, small, wide, wide, narrow, narrow),
        in_specs=[vmem, vmem, vmem, hbm, hbm],
        out_specs=(vmem, vmem, hbm, hbm, vmem, vmem),
        scratch_shapes=[
            pltpu.VMEM(w_up.shape, BF16),
            pltpu.VMEM(w_down.shape, BF16),
            pltpu.VMEM(inputs.shape, BF16),
            pltpu.VMEM(inputs.shape, BF16),
            pltpu.VMEM((jobs, 2, SIDE, toks, half), BF16),
            pltpu.VMEM((jobs, 2, tokens, half), BF16),
            pltpu.VMEM((2, CHUNKS, tokens, width), BF16),
            pltpu.VMEM((jobs, 2, CHUNKS, core_rows, width), BF16),
            pltpu.VMEM((jobs, 2, CHUNKS, core_rows, width), BF16),
            pltpu.VMEM((jobs, 2, CHUNKS, SIDE - 1, slab, width), BF16),
            pltpu.VMEM((jobs, 2, SIDE, toks, half), BF16),
            pltpu.VMEM((jobs, 2, SIDE - 1, toks, half), BF16),
            pltpu.VMEM((tokens, units), F32),
            pltpu.VMEM((tokens, units), F32),
            pltpu.VMEM((micro, tokens, units), F32),
            pltpu.VMEM((micro, tokens, units), F32),
            pltpu.VMEM((micro, toks, 128), F32),
            pltpu.VMEM((2, slab, half), F32),
            dma((2,)),
            dma((jobs, 2)),
            dma((2, micro)),
            dma((2, micro)),
            dma((jobs, 2)),
            dma((jobs, 2)),
            dma((jobs, 2)),
            dma((jobs, 2, SIDE - 1)),
            dma((jobs, 2)),
            dma((jobs, 2)),
            dma((jobs, 2, CHUNKS)),
            dma((jobs, 2, CHUNKS)),
            dma((jobs, 2, CHUNKS)),
            dma((jobs, 2, CHUNKS)),
            dma((jobs, 2)),
            dma((jobs, 2)),
        ],
        compiler_params=pltpu.CompilerParams(
            collective_id=0, has_side_effects=True, vmem_limit_bytes=VMEM_LIMIT
        ),
    )(inputs, cotangent, gain, w_up, w_down)


def shards(
    inputs, cotangent, gains, up_blocks, up_index, up_count, down_blocks, down_index, down_count
):
    features = inputs.shape[2]
    row_blocks = features // BLOCK
    group_blocks = FF // lax.axis_size("tp") // BLOCK
    w_up = densify(up_blocks[0], up_index[0], up_count[0, 0], row_blocks, group_blocks)
    w_down = densify(down_blocks[0], down_index[0], down_count[0, 0], group_blocks, row_blocks)
    outs, grads, normed, grad_rows, hidden, up_grad = layers(inputs, cotangent, gains, w_up, w_down)
    up_grads = weight_grad(normed, up_grad, up_index[0], up_count[0], True, group_blocks)
    down_grads = weight_grad(hidden, grad_rows, down_index[0], down_count[0], False, row_blocks)
    return (
        outs[None],
        grads[None],
        up_grads[None],
        down_grads[None],
    )


def solution(mesh):
    return jax.shard_map(
        shards,
        mesh=mesh,
        in_specs=(
            P(None, "tp", None),
            P(None, "tp", None),
            P("section", None),
            P("section", "tp", None),
            P("section", "tp"),
            P("section", "tp"),
            P("section", "tp", None),
            P("section", "tp"),
            P("section", "tp"),
        ),
        out_specs=(
            P("section", None, "tp", None),
            P("section", None, "tp", None),
            P("section", "tp", None),
            P("section", "tp", None),
        ),
        check_vma=False,
    )
```
